32 devices in a mesh: groups: 1, pairs: 4 (over z), chol: 4 (over y, x), walk: 2 (over core).
Axes of the slice: x: 2, y: 2, z: 4, core: 2. Of those that a mesh axis runs over, the one named last changes fastest.
Arguments:
- chol_vectors: bfloat16 [512, 768, 768], P(('groups', 'walk'), 'pairs', 'chol'), as said below
- trial_orbitals: float32 [768, 256], P('groups'), as said below
- walkers: float32 [16, 768, 256], P(('groups', 'pairs', 'chol'), None, 'walk'), as said below
- field_noise: float32 [1, 16, 512], P('groups', None, 'walk'), may hold values from -6 to 6
Outputs:
- propagated: float32 [16, 768, 256], P(('groups', 'pairs', 'chol'), None, 'walk')
- force_bias: float32 [1, 16, 512], P('groups', None, 'walk')
The draws below stay inside these ranges and needn't reach their ends.
Inputs may be any that keep to these rules, and one draw needn't show every extreme that they name: chol_vectors[g, p, q] = chol_vectors[g, q, p] for every g. The columns of trial_orbitals are linearly independent. `walkers`: every walker's intersection with trial_orbitals is far from singular.
All inputs are finite; a program needn't handle non-finite values.
Results may differ from the reference program's by a relative error of at most 0.0029.
Values may be sent and summed in bfloat16 or wider, within the bound.
No kernel may reach another device: no remote copies, remote signals or barrier semaphores. Data moves between devices by JAX's collectives and lax.ppermute only.
A program may use at most 64 MiB of HBM per device.

```python
import math
import jax
import jax.numpy as jnp
from jax import lax

ORBITALS = 768
ELECTRONS = 256
WINDOW = 512
STEPS = 1
TERMS = 6
WALKERS = 16


def draw_chol_vectors(key, part):
    spread = 0.7 / (0.05 * math.sqrt(WINDOW * ORBITALS))
    base = jax.random.truncated_normal(key, -4.0, 4.0, (WINDOW, ORBITALS, ORBITALS), jnp.float32)
    return ((base + jnp.swapaxes(base, 1, 2)) * (spread / math.sqrt(2.0))).astype(jnp.bfloat16)


def draw_trial_orbitals(key, part):
    return jax.random.truncated_normal(jax.random.fold_in(key, 11), -5.0, 5.0, (ORBITALS, ELECTRONS), jnp.float32)


def draw_walkers(key, part):
    trial_base = draw_trial_orbitals(key, part)
    offsets = jax.random.truncated_normal(jax.random.fold_in(key, 12), -4.0, 4.0, (WALKERS, ORBITALS, ELECTRONS), jnp.float32)
    return 1.5 * (trial_base[None, :, :] + offsets)


def levels(own_key, shape, shards, least, high):
    loudness = 1.0
    for dim, parts in shards:
        steps = jax.random.uniform(jax.random.fold_in(jax.random.fold_in(own_key, 6), dim), (parts,), jnp.float32, least / len(shards), high / len(shards))
        loudness = loudness * jnp.repeat(jnp.exp(steps), shape[dim] // parts).reshape((-1,) + (1,) * (len(shape) - 1 - dim))
    return loudness


def gaussian(key, dims, scale, bound, split=(), kind=jnp.bfloat16):
    values = scale * jax.random.normal(key, dims, jnp.float32)
    if split:
        values = values * levels(key, dims, split, -0.22, 0.18)
    return jnp.clip(values, -bound, bound).astype(kind)


def setup_inputs(seed: int = 0, part: int = 0) -> dict:
    key_of = jax.random.split(jax.random.key(seed), 5)
    part_splits = jax.random.split(jax.random.fold_in(key_of[4], part), 5)
    chol_vectors = draw_chol_vectors(jax.random.fold_in(jax.random.fold_in(key_of[4], part), 71), part)
    trial_orbitals = draw_trial_orbitals(jax.random.fold_in(jax.random.fold_in(key_of[4], part), 71), part)
    walkers = draw_walkers(jax.random.fold_in(jax.random.fold_in(key_of[4], part), 71), part)
    field_noise = gaussian(part_splits[3], (STEPS, WALKERS, WINDOW), 1.0, 6.0, ((2, 2),), jnp.float32)
    return {"chol_vectors": chol_vectors, "trial_orbitals": trial_orbitals, "walkers": walkers, "field_noise": field_noise}


root_step = 0.05
highest = lax.Precision.HIGHEST

def solve_normal(factor, right_side):
    middle = lax.linalg.triangular_solve(factor, right_side, left_side=True, lower=True)
    return lax.linalg.triangular_solve(factor, middle, left_side=True, lower=True, transpose_a=True)

def green_matrix(walker, trial_orbitals):
    intersection = jnp.dot(trial_orbitals.T, walker, precision=highest)
    normal = jnp.dot(intersection.T, intersection, precision=highest)
    factor = jnp.linalg.cholesky(normal)
    rotated = jnp.dot(intersection.T, trial_orbitals.T, precision=highest)
    solved = solve_normal(factor, rotated)
    return jnp.dot(walker, solved, precision=highest).astype(jnp.bfloat16)

def propagate(matrix, walker):
    running_term = walker
    running_sum = walker
    for degree in range(1, TERMS):
        running_term = -(root_step / degree) * jnp.dot(matrix, running_term, precision=highest)
        running_sum = running_sum + running_term
    return running_sum

def reference(chol_vectors, trial_orbitals, walkers, field_noise):
    flat_vectors = chol_vectors.reshape(WINDOW, ORBITALS * ORBITALS)
    block_size = math.gcd(WINDOW, 64)
    block_count = WINDOW // block_size
    propagated = walkers
    bias_steps = []
    for step_index in range(STEPS):
        greens = lax.map(lambda walker: green_matrix(walker, trial_orbitals), propagated)
        greens_flat = greens.reshape(WALKERS, ORBITALS * ORBITALS)
        force_bias = lax.dot_general(greens_flat.astype(jnp.float32), flat_vectors.astype(jnp.float32), (((1,), (1,)), ((), ())), preferred_element_type=jnp.float32)
        bias_steps.append(force_bias)
        shifted = field_noise[step_index] + root_step * force_bias

        def add_block(running, block_index):
            start_index = (block_index * block_size).astype(jnp.int32)
            chosen = lax.dynamic_slice_in_dim(flat_vectors, start_index, block_size, 0).astype(jnp.float32)
            weights = lax.dynamic_slice_in_dim(shifted, start_index, block_size, 1)
            return (running + jnp.dot(weights, chosen, precision=highest), None)
        potential = lax.scan(add_block, jnp.zeros((WALKERS, ORBITALS * ORBITALS), jnp.float32), jnp.arange(block_count, dtype=jnp.int32))[0]
        propagated = lax.map(lambda packed: propagate(packed[0].reshape(ORBITALS, ORBITALS), packed[1]), (potential, propagated))
    return (propagated, jnp.stack(bias_steps))
```

```python
import functools

import jax
import jax.numpy as jnp
from jax import lax
from jax.experimental import pallas as pl
from jax.experimental.pallas import tpu as pltpu
from jax.sharding import PartitionSpec as P

TERMS = 6


root_step = 0.05
highest = lax.Precision.HIGHEST
GROUP = 16
LANES = 128
f32 = jnp.float32
bf16 = jnp.bfloat16


def swapped(value, axis, apart):
    mask = 2**apart
    pairs = [(source, source ^ mask) for source in range(lax.axis_size(axis))]
    return lax.ppermute(value, axis, pairs)


def solve_normal(factor, right_side):
    middle = lax.linalg.triangular_solve(factor, right_side, left_side=True, lower=True)
    return lax.linalg.triangular_solve(factor, middle, left_side=True, lower=True, transpose_a=True)


def green_blocks(walker_full, trial_orbitals, trial_part, row_groups, col_groups):
    owner_walkers, orbital_count, electron_count = walker_full.shape
    intersection = jnp.einsum("nm,wnk->wmk", trial_orbitals, walker_full, precision=highest)
    normal = jnp.einsum("wmk,wml->wkl", intersection, intersection, precision=highest)
    factor = jnp.linalg.cholesky(normal)
    rotated = jnp.einsum("wmk,cbm->wkcb", intersection, trial_part, precision=highest)
    chosen_cols = rotated.shape[2] * rotated.shape[3]
    solved = solve_normal(factor, rotated.reshape(owner_walkers, electron_count, chosen_cols))
    slab_rows = orbital_count // row_groups
    block_cols = chosen_cols // col_groups
    shaped = solved.reshape(owner_walkers, electron_count, col_groups, block_cols)
    walker_rows = walker_full.reshape(owner_walkers, row_groups, slab_rows, electron_count)
    blocks = jnp.einsum("wiak,wkcb->icwab", walker_rows, shaped, precision=highest)
    return blocks.astype(jnp.bfloat16).reshape(
        row_groups * col_groups, owner_walkers, slab_rows * block_cols
    )


def shards(chol_vectors, trial_orbitals, walkers, field_noise):
    held_vectors, slab_rows, slab_cols = chol_vectors.shape
    owner_walkers = walkers.shape[0]
    orbital_count = walkers.shape[1]
    electron_count = trial_orbitals.shape[1]
    row_groups = lax.axis_size("pairs")
    col_groups = lax.axis_size("chol")
    core_count = lax.axis_size("walk")
    core_index = lax.axis_index("walk")
    core_cols = slab_cols // core_count
    owner_count = row_groups * col_groups
    walker_total = owner_count * owner_walkers
    flat_vectors = chol_vectors.reshape(held_vectors, slab_rows * slab_cols)
    trial_split = trial_orbitals.reshape(col_groups, core_count, core_cols, electron_count)
    trial_part = lax.dynamic_index_in_dim(trial_split, core_index, 1, keepdims=False)
    walker_full = lax.all_gather(walkers, "walk", axis=2, tiled=True)
    outgoing = green_blocks(walker_full, trial_orbitals, trial_part, row_groups, col_groups)
    sectioned = outgoing.reshape(row_groups, col_groups, owner_walkers, slab_rows * core_cols)
    arrived = lax.all_to_all(
        lax.all_to_all(sectioned, "pairs", split_axis=0, concat_axis=0, tiled=True),
        "chol",
        split_axis=1,
        concat_axis=1,
        tiled=True,
    )
    arrived = arrived.reshape(walker_total, slab_rows, core_cols)
    partial_bias = jnp.einsum(
        "wab,gab->wg",
        lax.all_gather(arrived, "walk", axis=2, tiled=True),
        chol_vectors,
        preferred_element_type=jnp.float32,
    )
    force_bias = lax.psum(partial_bias, ("pairs", "chol"))
    bias_steps = [force_bias]
    shifted = field_noise[0] + root_step * force_bias
    shifted_high = lax.optimization_barrier(shifted.astype(jnp.bfloat16))
    shifted_low = (shifted - shifted_high.astype(jnp.float32)).astype(jnp.bfloat16)
    stacked = jnp.stack([shifted_high, shifted_low])
    both_parts = lax.dot_general(
        stacked, flat_vectors, (((2,), (0,)), ((), ())), preferred_element_type=jnp.float32
    )
    potential = both_parts[0] + both_parts[1]
    blocks_out = potential.reshape(owner_count, owner_walkers, slab_rows * slab_cols)
    received = lax.all_to_all(
        blocks_out, ("pairs", "chol"), split_axis=0, concat_axis=0, tiled=True
    )
    partner = swapped(received, "walk", 0)
    summed = (received + partner).reshape(
        row_groups, col_groups, owner_walkers, slab_rows, core_count, core_cols
    )
    matrix = jnp.transpose(summed, (2, 0, 3, 1, 4, 5)).reshape(
        owner_walkers, orbital_count, orbital_count
    )
    running_term = walkers
    running_sum = walkers
    for degree in range(1, TERMS):
        running_term = -(root_step / degree) * jnp.einsum(
            "wpq,wqm->wpm", matrix, running_term, precision=highest
        )
        running_sum = running_sum + running_term
    return (running_sum, jnp.stack(bias_steps))


def split_two(value):
    high = value.astype(bf16)
    return high, (value - high.astype(f32)).astype(bf16)


def dot_of(left, right, dims=(((1,), (0,)), ((), ())), precision=None):
    return lax.dot_general(left, right, dims, precision=precision, preferred_element_type=f32)


def dot_three(left, right, dims=(((1,), (0,)), ((), ()))):
    left_high, left_low = split_two(left)
    right_high, right_low = split_two(right)
    return (
        dot_of(left_high, right_high, dims)
        + dot_of(left_high, right_low, dims)
        + dot_of(left_low, right_high, dims)
    )


first_dims = (((0,), (0,)), ((), ()))
last_dims = (((1,), (1,)), ((), ()))


def eye_of(size):
    rows = lax.broadcasted_iota(jnp.int32, (size, size), 0)
    cols = lax.broadcasted_iota(jnp.int32, (size, size), 1)
    return (rows == cols).astype(f32)


def half_rolled(value):
    return pltpu.roll(value, LANES // 2, 1)


def tail_lanes(value):
    return lax.broadcasted_iota(jnp.int32, value.shape, 1) < LANES // 2


LOW_START = 5e-4
PAIRED_STEPS = 6
RESIDUAL_BOUND = 3e-3
MOST_STEPS = 60


def scales():
    low = LOW_START
    found = []
    for _ in range(PAIRED_STEPS + 1):
        scale = 2.0 / (1.0 + 2.0 * low - low * low)
        found.append(scale)
        low = 2.0 - scale
    return found


def green_body(core_ref, own_ref, other_ref, trial_ref, out_ref, inverse_ref, matrix_ref, *, row_groups, col_groups):
    orbital_count, electron_count = trial_ref.shape
    slab_rows = orbital_count // row_groups
    slab_cols = orbital_count // col_groups
    core = core_ref[0]
    half = slab_rows // 2
    walker = jnp.concatenate([own_ref[...], other_ref[...]], axis=1)
    trial = trial_ref[...]
    inter = dot_of(trial, walker, first_dims, highest)
    inverse_scale = 1.0 / jnp.max(jnp.abs(inter))
    inter = inter * inverse_scale
    matrix_ref[...] = inter
    turned = inter.T
    eye = eye_of(electron_count)
    normal = dot_three(turned, inter)
    both = dot_three(normal, jnp.concatenate([normal, turned], axis=1))
    square = both[:, :electron_count]
    step_scales = scales()
    largest = jnp.sqrt(jnp.sqrt(jnp.sum(square * square))) * 1.001
    alpha = (2.0 - LOW_START) / largest
    scale = step_scales[0]
    error = eye - (2.0 * scale * alpha) * normal + (scale * alpha * alpha) * square
    inverse = (scale * alpha) * (2.0 * turned - alpha * both[:, electron_count:])
    for scale in step_scales[1:]:
        both = dot_three(error, jnp.concatenate([error, inverse], axis=1))
        inverse = scale * (inverse + both[:, electron_count:])
        error = (1.0 - scale) * eye + scale * both[:, :electron_count]
    inverse_ref[...] = inverse

    def refine(carried):
        count, _ = carried
        current = inverse_ref[...]
        residual = eye_of(electron_count) - dot_of(current, matrix_ref[...], precision=highest)
        inverse_ref[...] = current + dot_three(residual, current)
        return count + 1, jnp.sum(residual * residual)

    lax.while_loop(
        lambda carried: jnp.logical_and(carried[0] < MOST_STEPS, carried[1] > RESIDUAL_BOUND**2),
        refine,
        (jnp.int32(0), jnp.float32(1e30)),
    )
    chosen = []
    for row in range(row_groups):
        start = pl.multiple_of(row * slab_rows + core * half, 8)
        chosen.append(
            jnp.concatenate(
                [own_ref[pl.ds(start, half), :], other_ref[pl.ds(start, half), :]], axis=1
            )
        )
    scaled = dot_three(jnp.concatenate(chosen, axis=0), inverse_ref[...]) * inverse_scale
    pieces = [trial_ref[slab_cols * c : slab_cols * c + LANES, :] for c in range(col_groups)]
    pieces += [trial_ref[slab_cols * c + LANES : slab_cols * (c + 1), :] for c in range(col_groups)]
    green = dot_three(scaled, jnp.concatenate(pieces, axis=0), last_dims)
    quarter = half // 2
    for row in range(row_groups):
        for col in range(col_groups):
            place = row * col_groups + col
            slab = green[row * half : (row + 1) * half]
            out_ref[place, 0:half, :] = slab[:, col * LANES : (col + 1) * LANES].astype(bf16)
            start = (col_groups + col // 2) * LANES
            top = slab[:quarter, start : start + LANES]
            bottom = slab[quarter:, start : start + LANES]
            if col % 2 == 0:
                packed = jnp.where(tail_lanes(top), top, half_rolled(bottom))
            else:
                packed = jnp.where(tail_lanes(top), half_rolled(top), bottom)
            out_ref[place, half : half + quarter, :] = packed.astype(bf16)


def bias_body(core_ref, own_ref, other_ref, vector_ref, out_ref, green_ref, sums_ref, *, slab_rows, slab_cols):
    step = pl.program_id(0)
    walker_total = own_ref.shape[0]
    block = vector_ref.shape[0]
    half = slab_rows // 2
    groups = half // GROUP
    wide = walker_total * GROUP

    @pl.when(step == 0)
    def _():
        core = core_ref[0]
        for source, place in ((own_ref, core), (other_ref, 1 - core)):
            for group in range(groups):
                main = source[:, group * GROUP : (group + 1) * GROUP, :].reshape(wide, LANES)
                start = half + (group % (groups // 2)) * GROUP
                tail = source[:, start : start + GROUP, :].reshape(wide, LANES)
                if group >= groups // 2:
                    tail = half_rolled(tail.astype(f32)).astype(bf16)
                green_ref[place * groups + group, :, 0:LANES] = main
                green_ref[place * groups + group, :, LANES:slab_cols] = tail[:, 0 : slab_cols - LANES]

    total = jnp.zeros((block * GROUP, wide), f32)
    for group in range(slab_rows // GROUP):
        chosen = vector_ref[:, group * GROUP : (group + 1) * GROUP, :]
        total = total + dot_of(chosen.reshape(block * GROUP, slab_cols), green_ref[group], last_dims)
    rows = lax.broadcasted_iota(jnp.int32, total.shape, 0) % GROUP
    cols = lax.broadcasted_iota(jnp.int32, total.shape, 1) % GROUP
    kept = jnp.where(rows == cols, total, 0.0)
    start = pl.multiple_of(step * block, block)
    sums_ref[pl.ds(start, block), :] = kept.reshape(block, GROUP, wide).sum(axis=1)

    @pl.when(step == pl.num_programs(0) - 1)
    def _():
        owner = lax.broadcasted_iota(jnp.int32, (walker_total, wide), 0)
        place = lax.broadcasted_iota(jnp.int32, (walker_total, wide), 1) // GROUP
        bias = dot_of((owner == place).astype(f32), sums_ref[...], last_dims, highest)
        for device in range(out_ref.shape[0]):
            out_ref[device] = bias


def potential_body(core_ref, parts_ref, noise_ref, vector_ref, bias_ref, keep_ref, send_ref, weights_ref, mixed_ref, total_ref, *, slab_rows, slab_cols):
    step = pl.program_id(0)
    walker_total, held = noise_ref.shape
    block = vector_ref.shape[0]
    wide = walker_total * GROUP
    half = slab_rows // 2
    groups = half // GROUP

    @pl.when(step == 0)
    def _():
        bias = parts_ref[0]
        for device in range(1, parts_ref.shape[0]):
            bias = bias + parts_ref[device]
        bias_ref[...] = bias
        shifted = noise_ref[...] + root_step * bias
        spread = jnp.broadcast_to(shifted[:, None, :], (walker_total, GROUP, held)).reshape(wide, held)
        high, low = split_two(spread)
        weights_ref[0:wide, :] = high
        weights_ref[wide : 2 * wide, :] = low

    source = lax.broadcasted_iota(jnp.int32, (held, block * GROUP), 0)
    target = lax.broadcasted_iota(jnp.int32, (held, block * GROUP), 1)
    chooser = (source == step * block + target // GROUP).astype(bf16)
    mixed = dot_of(weights_ref[...], chooser)
    rows = lax.broadcasted_iota(jnp.int32, mixed.shape, 0) % GROUP
    cols = lax.broadcasted_iota(jnp.int32, mixed.shape, 1) % GROUP
    mixed_ref[...] = jnp.where(rows == cols, mixed, 0.0).astype(bf16)
    for group in range(slab_rows // GROUP):
        chosen = vector_ref[:, group * GROUP : (group + 1) * GROUP, :]
        both = dot_of(mixed_ref[...], chosen.reshape(block * GROUP, slab_cols))
        added = both[:wide] + both[wide:]

        @pl.when(step == 0)
        def _():
            total_ref[group] = added

        @pl.when(step > 0)
        def _():
            total_ref[group] = total_ref[group] + added

    @pl.when(step == pl.num_programs(0) - 1)
    def _():
        core = core_ref[0]
        shape = (walker_total, GROUP, LANES)
        for target_ref, place in ((keep_ref, core), (send_ref, 1 - core)):
            for group in range(groups):
                value = total_ref[place * groups + group]
                target_ref[:, group * GROUP : (group + 1) * GROUP, :] = value[:, :LANES].reshape(shape)
                if group < groups // 2:
                    paired = total_ref[place * groups + group + groups // 2]
                    tail = jnp.concatenate([value[:, LANES:], paired[:, LANES:]], axis=1)
                    start = half + group * GROUP
                    target_ref[:, start : start + GROUP, :] = tail.reshape(shape)


def series_body(core_ref, own_ref, other_ref, walker_ref, out_ref, matrix_ref, *, row_groups, col_groups):
    orbital_count = walker_ref.shape[0]
    slab_rows = orbital_count // row_groups
    slab_cols = orbital_count // col_groups
    half = slab_rows // 2
    quarter = half // 2
    core = core_ref[0]
    for source, place in ((own_ref, core), (other_ref, 1 - core)):
        for row in range(row_groups):
            start = pl.multiple_of(row * slab_rows + place * half, GROUP)
            for col in range(col_groups):
                index = row * col_groups + col
                matrix_ref[pl.ds(start, half), col * LANES : (col + 1) * LANES] = source[index, 0:half, :]
            for col in range(0, col_groups, 2):
                index = row * col_groups + col
                even = source[index, half : half + quarter, :].astype(f32)
                odd = source[index + 1, half : half + quarter, :].astype(f32)
                top = jnp.where(tail_lanes(even), even, half_rolled(odd))
                bottom = jnp.where(tail_lanes(even), half_rolled(even), odd)
                lane = (col_groups + col // 2) * LANES
                joined = jnp.concatenate([top, bottom], axis=0).astype(bf16)
                matrix_ref[pl.ds(start, half), lane : lane + LANES] = joined

    term = walker_ref[...]
    total = term
    width = term.shape[1]
    for degree in range(1, TERMS):
        order = [term[slab_cols * c : slab_cols * c + LANES] for c in range(col_groups)]
        order += [term[slab_cols * c + LANES : slab_cols * (c + 1)] for c in range(col_groups)]
        high, low = split_two(jnp.concatenate(order, axis=0))
        both = dot_of(matrix_ref[...], jnp.concatenate([high, low], axis=1))
        term = (-root_step / degree) * (both[:, :width] + both[:, width:])
        total = total + term
    out_ref[...] = total


smem = pl.BlockSpec(memory_space=pltpu.SMEM)
vmem = pl.BlockSpec(memory_space=pltpu.VMEM)
BLOCK = 32


def fast_shards(chol_vectors, trial_orbitals, walkers, field_noise):
    held, slab_rows, slab_cols = chol_vectors.shape
    orbital_count, electron_count = trial_orbitals.shape
    row_groups = lax.axis_size("pairs")
    col_groups = lax.axis_size("chol")
    owners = row_groups * col_groups
    half = slab_rows // 2
    dense = half + half // 2
    wide = owners * GROUP
    core = lax.axis_index("walk").astype(jnp.int32).reshape(1)
    own = walkers[0]
    other = swapped(own, "walk", 0)
    outgoing = pl.pallas_call(
        functools.partial(green_body, row_groups=row_groups, col_groups=col_groups),
        out_shape=jax.ShapeDtypeStruct((owners, dense, LANES), bf16),
        in_specs=[smem, vmem, vmem, vmem],
        out_specs=vmem,
        scratch_shapes=[pltpu.VMEM((electron_count, electron_count), f32)] * 2,
        name="green",
    )(core, own, other, trial_orbitals)
    axes = ("pairs", "chol")
    arrived = lax.all_to_all(outgoing, axes, split_axis=0, concat_axis=0, tiled=True)
    arrived_other = swapped(arrived, "walk", 0)
    blocks = pl.BlockSpec((BLOCK, slab_rows, slab_cols), lambda step: (step, 0, 0))
    spread = pl.pallas_call(
        functools.partial(bias_body, slab_rows=slab_rows, slab_cols=slab_cols),
        grid=(held // BLOCK,),
        out_shape=jax.ShapeDtypeStruct((owners, owners, held), f32),
        in_specs=[smem, vmem, vmem, blocks],
        out_specs=vmem,
        scratch_shapes=[
            pltpu.VMEM((slab_rows // GROUP, wide, slab_cols), bf16),
            pltpu.VMEM((held, wide), f32),
        ],
        name="bias",
    )(core, arrived, arrived_other, chol_vectors)
    parts = lax.all_to_all(spread, axes, split_axis=0, concat_axis=0, tiled=True)
    force_bias, keep, send = pl.pallas_call(
        functools.partial(potential_body, slab_rows=slab_rows, slab_cols=slab_cols),
        grid=(held // BLOCK,),
        out_shape=(
            jax.ShapeDtypeStruct((owners, held), f32),
            jax.ShapeDtypeStruct((owners, dense, LANES), f32),
            jax.ShapeDtypeStruct((owners, dense, LANES), f32),
        ),
        in_specs=[smem, vmem, vmem, blocks],
        out_specs=(vmem, vmem, vmem),
        scratch_shapes=[
            pltpu.VMEM((2 * wide, held), bf16),
            pltpu.VMEM((2 * wide, BLOCK * GROUP), bf16),
            pltpu.VMEM((slab_rows // GROUP, wide, slab_cols), f32),
        ],
        name="potential",
    )(core, parts, field_noise[0], chol_vectors)
    summed = (keep + swapped(send, "walk", 0)).astype(bf16)
    received = lax.all_to_all(summed, axes, split_axis=0, concat_axis=0, tiled=True)
    received_other = swapped(received, "walk", 0)
    propagated = pl.pallas_call(
        functools.partial(series_body, row_groups=row_groups, col_groups=col_groups),
        out_shape=jax.ShapeDtypeStruct(own.shape, f32),
        in_specs=[smem, vmem, vmem, vmem],
        out_specs=vmem,
        scratch_shapes=[pltpu.VMEM((orbital_count, orbital_count), bf16)],
        name="series",
    )(core, received, received_other, own)
    return propagated[None], force_bias[None]


def packable(chol_vectors, trial_orbitals, walkers, field_noise):
    held, slab_rows, slab_cols = chol_vectors.shape
    owners = lax.axis_size("pairs") * lax.axis_size("chol")
    return (
        walkers.shape[0] == 1
        and owners * GROUP <= 512
        and lax.axis_size("walk") == 2
        and lax.axis_size("chol") % 2 == 0
        and slab_cols == LANES + LANES // 2
        and slab_rows % (4 * GROUP) == 0
        and held % BLOCK == 0
        and trial_orbitals.shape[1] % 256 == 0
        and field_noise.shape[0] == 1
    )


def chosen_shards(*args):
    return fast_shards(*args) if packable(*args) else shards(*args)


def solution(mesh):
    placed = (
        P(("groups", "walk"), "pairs", "chol"),
        P("groups", None),
        P(("groups", "pairs", "chol"), None, "walk"),
        P("groups", None, "walk"),
    )
    return jax.shard_map(
        chosen_shards,
        mesh=mesh,
        in_specs=placed,
        out_specs=(P(("groups", "pairs", "chol"), None, "walk"), P("groups", None, "walk")),
        check_vma=False,
    )
```

```python
import functools

import jax
import jax.numpy as jnp
from jax import lax
from jax.experimental import pallas as pl
from jax.experimental.pallas import tpu as pltpu
from jax.sharding import PartitionSpec as P

TERMS = 6


root_step = 0.05
highest = lax.Precision.HIGHEST
GROUP = 16
LANES = 128
f32 = jnp.float32
bf16 = jnp.bfloat16


def swapped(value, axis, apart):
    mask = 2**apart
    pairs = [(source, source ^ mask) for source in range(lax.axis_size(axis))]
    return lax.ppermute(value, axis, pairs)


def solve_normal(factor, right_side):
    middle = lax.linalg.triangular_solve(factor, right_side, left_side=True, lower=True)
    return lax.linalg.triangular_solve(factor, middle, left_side=True, lower=True, transpose_a=True)


def green_blocks(walker_full, trial_orbitals, trial_part, row_groups, col_groups):
    owner_walkers, orbital_count, electron_count = walker_full.shape
    intersection = jnp.einsum("nm,wnk->wmk", trial_orbitals, walker_full, precision=highest)
    normal = jnp.einsum("wmk,wml->wkl", intersection, intersection, precision=highest)
    factor = jnp.linalg.cholesky(normal)
    rotated = jnp.einsum("wmk,cbm->wkcb", intersection, trial_part, precision=highest)
    chosen_cols = rotated.shape[2] * rotated.shape[3]
    solved = solve_normal(factor, rotated.reshape(owner_walkers, electron_count, chosen_cols))
    slab_rows = orbital_count // row_groups
    block_cols = chosen_cols // col_groups
    shaped = solved.reshape(owner_walkers, electron_count, col_groups, block_cols)
    walker_rows = walker_full.reshape(owner_walkers, row_groups, slab_rows, electron_count)
    blocks = jnp.einsum("wiak,wkcb->icwab", walker_rows, shaped, precision=highest)
    return blocks.astype(jnp.bfloat16).reshape(
        row_groups * col_groups, owner_walkers, slab_rows * block_cols
    )


def shards(chol_vectors, trial_orbitals, walkers, field_noise):
    held_vectors, slab_rows, slab_cols = chol_vectors.shape
    owner_walkers = walkers.shape[0]
    orbital_count = walkers.shape[1]
    electron_count = trial_orbitals.shape[1]
    row_groups = lax.axis_size("pairs")
    col_groups = lax.axis_size("chol")
    core_count = lax.axis_size("walk")
    core_index = lax.axis_index("walk")
    core_cols = slab_cols // core_count
    owner_count = row_groups * col_groups
    walker_total = owner_count * owner_walkers
    flat_vectors = chol_vectors.reshape(held_vectors, slab_rows * slab_cols)
    trial_split = trial_orbitals.reshape(col_groups, core_count, core_cols, electron_count)
    trial_part = lax.dynamic_index_in_dim(trial_split, core_index, 1, keepdims=False)
    walker_full = lax.all_gather(walkers, "walk", axis=2, tiled=True)
    outgoing = green_blocks(walker_full, trial_orbitals, trial_part, row_groups, col_groups)
    sectioned = outgoing.reshape(row_groups, col_groups, owner_walkers, slab_rows * core_cols)
    arrived = lax.all_to_all(
        lax.all_to_all(sectioned, "pairs", split_axis=0, concat_axis=0, tiled=True),
        "chol",
        split_axis=1,
        concat_axis=1,
        tiled=True,
    )
    arrived = arrived.reshape(walker_total, slab_rows, core_cols)
    partial_bias = jnp.einsum(
        "wab,gab->wg",
        lax.all_gather(arrived, "walk", axis=2, tiled=True),
        chol_vectors,
        preferred_element_type=jnp.float32,
    )
    force_bias = lax.psum(partial_bias, ("pairs", "chol"))
    bias_steps = [force_bias]
    shifted = field_noise[0] + root_step * force_bias
    shifted_high = lax.optimization_barrier(shifted.astype(jnp.bfloat16))
    shifted_low = (shifted - shifted_high.astype(jnp.float32)).astype(jnp.bfloat16)
    stacked = jnp.stack([shifted_high, shifted_low])
    both_parts = lax.dot_general(
        stacked, flat_vectors, (((2,), (0,)), ((), ())), preferred_element_type=jnp.float32
    )
    potential = both_parts[0] + both_parts[1]
    blocks_out = potential.reshape(owner_count, owner_walkers, slab_rows * slab_cols)
    received = lax.all_to_all(
        blocks_out, ("pairs", "chol"), split_axis=0, concat_axis=0, tiled=True
    )
    partner = swapped(received, "walk", 0)
    summed = (received + partner).reshape(
        row_groups, col_groups, owner_walkers, slab_rows, core_count, core_cols
    )
    matrix = jnp.transpose(summed, (2, 0, 3, 1, 4, 5)).reshape(
        owner_walkers, orbital_count, orbital_count
    )
    running_term = walkers
    running_sum = walkers
    for degree in range(1, TERMS):
        running_term = -(root_step / degree) * jnp.einsum(
            "wpq,wqm->wpm", matrix, running_term, precision=highest
        )
        running_sum = running_sum + running_term
    return (running_sum, jnp.stack(bias_steps))


def split_two(value):
    high = value.astype(bf16)
    return high, (value - high.astype(f32)).astype(bf16)


def dot_of(left, right, dims=(((1,), (0,)), ((), ())), precision=None):
    return lax.dot_general(left, right, dims, precision=precision, preferred_element_type=f32)


def dot_three(left, right, dims=(((1,), (0,)), ((), ()))):
    left_high, left_low = split_two(left)
    right_high, right_low = split_two(right)
    return (
        dot_of(left_high, right_high, dims)
        + dot_of(left_high, right_low, dims)
        + dot_of(left_low, right_high, dims)
    )


first_dims = (((0,), (0,)), ((), ()))
last_dims = (((1,), (1,)), ((), ()))


def eye_of(size):
    rows = lax.broadcasted_iota(jnp.int32, (size, size), 0)
    cols = lax.broadcasted_iota(jnp.int32, (size, size), 1)
    return (rows == cols).astype(f32)


def half_rolled(value):
    return pltpu.roll(value, LANES // 2, 1)


def tail_lanes(value):
    return lax.broadcasted_iota(jnp.int32, value.shape, 1) < LANES // 2


LOW_START = 5e-4
PAIRED_STEPS = 6
RESIDUAL_BOUND = 3e-3
MOST_STEPS = 60


def scales():
    low = LOW_START
    found = []
    for _ in range(PAIRED_STEPS + 1):
        scale = 2.0 / (1.0 + 2.0 * low - low * low)
        found.append(scale)
        low = 2.0 - scale
    return found


def green_body(core_ref, own_ref, other_ref, trial_ref, out_ref, inverse_ref, matrix_ref, *, row_groups, col_groups):
    orbital_count, electron_count = trial_ref.shape
    slab_rows = orbital_count // row_groups
    slab_cols = orbital_count // col_groups
    core = core_ref[0]
    half = slab_rows // 2
    walker = jnp.concatenate([own_ref[...], other_ref[...]], axis=1)
    trial = trial_ref[...]
    inter = dot_of(trial, walker, first_dims, highest)
    inverse_scale = 1.0 / jnp.max(jnp.abs(inter))
    inter = inter * inverse_scale
    matrix_ref[...] = inter
    turned = inter.T
    eye = eye_of(electron_count)
    normal = dot_three(turned, inter)
    both = dot_three(normal, jnp.concatenate([normal, turned], axis=1))
    square = both[:, :electron_count]
    step_scales = scales()
    largest = jnp.sqrt(jnp.sqrt(jnp.sum(square * square))) * 1.001
    alpha = (2.0 - LOW_START) / largest
    scale = step_scales[0]
    error = eye - (2.0 * scale * alpha) * normal + (scale * alpha * alpha) * square
    inverse = (scale * alpha) * (2.0 * turned - alpha * both[:, electron_count:])
    for scale in step_scales[1:]:
        both = dot_three(error, jnp.concatenate([error, inverse], axis=1))
        inverse = scale * (inverse + both[:, electron_count:])
        error = (1.0 - scale) * eye + scale * both[:, :electron_count]
    inverse_ref[...] = inverse

    def refine(carried):
        count, _ = carried
        current = inverse_ref[...]
        residual = eye_of(electron_count) - dot_of(current, matrix_ref[...], precision=highest)
        inverse_ref[...] = current + dot_three(residual, current)
        return count + 1, jnp.sum(residual * residual)

    lax.while_loop(
        lambda carried: jnp.logical_and(carried[0] < MOST_STEPS, carried[1] > RESIDUAL_BOUND**2),
        refine,
        (jnp.int32(0), jnp.float32(1e30)),
    )
    chosen = []
    for row in range(row_groups):
        start = pl.multiple_of(row * slab_rows + core * half, 8)
        chosen.append(
            jnp.concatenate(
                [own_ref[pl.ds(start, half), :], other_ref[pl.ds(start, half), :]], axis=1
            )
        )
    scaled = dot_three(jnp.concatenate(chosen, axis=0), inverse_ref[...]) * inverse_scale
    pieces = [trial_ref[slab_cols * c : slab_cols * c + LANES, :] for c in range(col_groups)]
    pieces += [trial_ref[slab_cols * c + LANES : slab_cols * (c + 1), :] for c in range(col_groups)]
    green = dot_three(scaled, jnp.concatenate(pieces, axis=0), last_dims)
    quarter = half // 2
    for row in range(row_groups):
        for col in range(col_groups):
            place = row * col_groups + col
            slab = green[row * half : (row + 1) * half]
            out_ref[place, 0:half, :] = slab[:, col * LANES : (col + 1) * LANES].astype(bf16)
            start = (col_groups + col // 2) * LANES
            tails = slab[:, start : start + LANES].reshape(-1, 2, GROUP // 2, LANES)
            top = tails[:, 0].reshape(quarter, LANES)
            bottom = tails[:, 1].reshape(quarter, LANES)
            if col % 2 == 0:
                packed = jnp.where(tail_lanes(top), top, half_rolled(bottom))
            else:
                packed = jnp.where(tail_lanes(top), half_rolled(top), bottom)
            out_ref[place, half : half + quarter, :] = packed.astype(bf16)


def packed_rows(vector_ref, group):
    chosen = vector_ref[group * GROUP : (group + 1) * GROUP]
    pieces = [chosen[row, :LANES] for row in range(GROUP)]
    for row in range(GROUP // 2):
        pieces += [chosen[row, LANES:], chosen[row + GROUP // 2, LANES:]]
    return jnp.concatenate(pieces, axis=0)


def bias_body(place_ref, green_ref, vector_ref, before_ref, out_ref, turned_ref, total_ref):
    step = pl.program_id(0)
    groups = vector_ref.shape[0] // GROUP
    half = pl.num_programs(0) * groups * GROUP

    @pl.when(step == 0)
    def _():
        turned_ref[...] = jnp.swapaxes(green_ref[...].astype(f32), 0, 1).astype(bf16)
        total_ref[...] = before_ref[...]

    total = total_ref[...]
    for group in range(groups):
        index = step * groups + group
        pieces = [turned_ref[index * GROUP + row] for row in range(GROUP)]
        pieces += [turned_ref[half + index * (GROUP // 2) + row] for row in range(GROUP // 2)]
        total = total + dot_of(jnp.concatenate(pieces, axis=1), packed_rows(vector_ref, group))
    total_ref[...] = total

    @pl.when(step == pl.num_programs(0) - 1)
    def _():
        for device in range(out_ref.shape[0]):
            out_ref[device] = total_ref[...]


def potential_body(place_ref, parts_ref, noise_ref, vector_ref, bias_ref, out_ref, weights_ref):
    step = pl.program_id(0)
    walker_total = noise_ref.shape[0]
    groups = vector_ref.shape[0] // GROUP
    half = pl.num_programs(0) * groups * GROUP

    @pl.when(step == 0)
    def _():
        bias = parts_ref[0]
        for device in range(1, parts_ref.shape[0]):
            bias = bias + parts_ref[device]
        bias_ref[...] = bias
        high, low = split_two(noise_ref[...] + root_step * bias)
        weights_ref[...] = jnp.concatenate([high, low], axis=0)

    for group in range(groups):
        index = step * groups + group
        both = dot_of(weights_ref[...], packed_rows(vector_ref, group), last_dims)
        added = both[:walker_total] + both[walker_total:]
        for row in range(GROUP):
            out_ref[index * GROUP + row] = added[:, row * LANES : (row + 1) * LANES]
        for row in range(GROUP // 2):
            start = (GROUP + row) * LANES
            out_ref[half + index * (GROUP // 2) + row] = added[:, start : start + LANES]


def series_body(core_ref, own_ref, other_ref, walker_ref, out_ref, matrix_ref, *, row_groups, col_groups):
    orbital_count = walker_ref.shape[0]
    slab_rows = orbital_count // row_groups
    slab_cols = orbital_count // col_groups
    half = slab_rows // 2
    quarter = half // 2
    core = core_ref[0]
    for source, place in ((own_ref, core), (other_ref, 1 - core)):
        for row in range(row_groups):
            start = pl.multiple_of(row * slab_rows + place * half, GROUP)
            for col in range(col_groups):
                index = row * col_groups + col
                matrix_ref[pl.ds(start, half), col * LANES : (col + 1) * LANES] = source[index, 0:half, :]
            for col in range(0, col_groups, 2):
                index = row * col_groups + col
                even = source[index, half : half + quarter, :].astype(f32)
                odd = source[index + 1, half : half + quarter, :].astype(f32)
                top = jnp.where(tail_lanes(even), even, half_rolled(odd))
                bottom = jnp.where(tail_lanes(even), half_rolled(even), odd)
                lane = (col_groups + col // 2) * LANES
                parts = [part.reshape(-1, 1, GROUP // 2, LANES) for part in (top, bottom)]
                joined = jnp.concatenate(parts, axis=1).reshape(half, LANES).astype(bf16)
                matrix_ref[pl.ds(start, half), lane : lane + LANES] = joined

    term = walker_ref[...]
    total = term
    width = term.shape[1]
    for degree in range(1, TERMS):
        order = [term[slab_cols * c : slab_cols * c + LANES] for c in range(col_groups)]
        order += [term[slab_cols * c + LANES : slab_cols * (c + 1)] for c in range(col_groups)]
        high, low = split_two(jnp.concatenate(order, axis=0))
        both = dot_of(matrix_ref[...], jnp.concatenate([high, low], axis=1))
        term = (-root_step / degree) * (both[:, :width] + both[:, width:])
        total = total + term
    out_ref[...] = total


smem = pl.BlockSpec(memory_space=pltpu.SMEM)
vmem = pl.BlockSpec(memory_space=pltpu.VMEM)
BLOCK = 32


def bias_half(place, green, vectors, before, copies):
    owners, dense, _ = green.shape
    slab_rows, slab_cols, held = vectors.shape
    steps = slab_rows // 2 // BLOCK
    whole = lambda *shape: pl.BlockSpec(shape, lambda step, place: (0,) * len(shape))
    return pl.pallas_call(
        bias_body,
        grid_spec=pltpu.PrefetchScalarGridSpec(
            num_scalar_prefetch=1,
            grid=(steps,),
            in_specs=[
                whole(owners, dense, LANES),
                pl.BlockSpec(
                    (BLOCK, slab_cols, held), lambda step, place: (place[0] * steps + step, 0, 0)
                ),
                whole(owners, held),
            ],
            out_specs=whole(copies, owners, held),
            scratch_shapes=[
                pltpu.VMEM((dense, owners, LANES), bf16),
                pltpu.VMEM((owners, held), f32),
            ],
        ),
        out_shape=jax.ShapeDtypeStruct((copies, owners, held), f32),
        name="bias",
    )(place, green, vectors, before)


def potential_half(place, parts, noise, vectors):
    count, owners, held = parts.shape
    slab_rows, slab_cols, _ = vectors.shape
    dense = slab_rows // 2 * 3 // 2
    steps = slab_rows // 2 // BLOCK
    whole = lambda *shape: pl.BlockSpec(shape, lambda step, place: (0,) * len(shape))
    return pl.pallas_call(
        potential_body,
        grid_spec=pltpu.PrefetchScalarGridSpec(
            num_scalar_prefetch=1,
            grid=(steps,),
            in_specs=[
                whole(count, owners, held),
                whole(owners, held),
                pl.BlockSpec(
                    (BLOCK, slab_cols, held), lambda step, place: (place[0] * steps + step, 0, 0)
                ),
            ],
            out_specs=(whole(owners, held), whole(dense, owners, LANES)),
            scratch_shapes=[pltpu.VMEM((2 * owners, held), bf16)],
        ),
        out_shape=(
            jax.ShapeDtypeStruct((owners, held), f32),
            jax.ShapeDtypeStruct((dense, owners, LANES), f32),
        ),
        name="potential",
    )(place, parts, noise, vectors)


def fast_shards(chol_vectors, trial_orbitals, walkers, field_noise):
    held, slab_rows, slab_cols = chol_vectors.shape
    orbital_count, electron_count = trial_orbitals.shape
    row_groups = lax.axis_size("pairs")
    col_groups = lax.axis_size("chol")
    owners = row_groups * col_groups
    dense = slab_rows // 2 * 3 // 2
    core = lax.axis_index("walk").astype(jnp.int32).reshape(1)
    vectors = jnp.transpose(chol_vectors, (1, 2, 0))
    own = walkers[0]
    other = swapped(own, "walk", 0)
    outgoing = pl.pallas_call(
        functools.partial(green_body, row_groups=row_groups, col_groups=col_groups),
        out_shape=jax.ShapeDtypeStruct((owners, dense, LANES), bf16),
        in_specs=[smem, vmem, vmem, vmem],
        out_specs=vmem,
        scratch_shapes=[pltpu.VMEM((electron_count, electron_count), f32)] * 2,
        name="green",
    )(core, own, other, trial_orbitals)
    axes = ("pairs", "chol")
    arrived = lax.all_to_all(outgoing, axes, split_axis=0, concat_axis=0, tiled=True)
    arrived_other = swapped(arrived, "walk", 0)
    first = bias_half(core, arrived, vectors, jnp.zeros((owners, held), f32), 1)
    spread = bias_half(1 - core, arrived_other, vectors, first[0], owners)
    parts = lax.all_to_all(spread, axes, split_axis=0, concat_axis=0, tiled=True)
    force_bias, send = potential_half(1 - core, parts, field_noise[0], vectors)
    _, keep = potential_half(core, parts, field_noise[0], vectors)
    summed = jnp.swapaxes((keep + swapped(send, "walk", 0)).astype(bf16), 0, 1)
    received = lax.all_to_all(summed, axes, split_axis=0, concat_axis=0, tiled=True)
    received_other = swapped(received, "walk", 0)
    propagated = pl.pallas_call(
        functools.partial(series_body, row_groups=row_groups, col_groups=col_groups),
        out_shape=jax.ShapeDtypeStruct(own.shape, f32),
        in_specs=[smem, vmem, vmem, vmem],
        out_specs=vmem,
        scratch_shapes=[pltpu.VMEM((orbital_count, orbital_count), bf16)],
        name="series",
    )(core, received, received_other, own)
    return propagated[None], force_bias[None]


def packable(chol_vectors, trial_orbitals, walkers, field_noise):
    held, slab_rows, slab_cols = chol_vectors.shape
    owners = lax.axis_size("pairs") * lax.axis_size("chol")
    return (
        walkers.shape[0] == 1
        and owners * GROUP <= 512
        and lax.axis_size("walk") == 2
        and lax.axis_size("chol") % 2 == 0
        and slab_cols == LANES + LANES // 2
        and slab_rows % (2 * BLOCK) == 0
        and trial_orbitals.shape[1] % 256 == 0
        and field_noise.shape[0] == 1
    )


def chosen_shards(*args):
    return fast_shards(*args) if packable(*args) else shards(*args)


def solution(mesh):
    placed = (
        P(("groups", "walk"), "pairs", "chol"),
        P("groups", None),
        P(("groups", "pairs", "chol"), None, "walk"),
        P("groups", None, "walk"),
    )
    return jax.shard_map(
        chosen_shards,
        mesh=mesh,
        in_specs=placed,
        out_specs=(P(("groups", "pairs", "chol"), None, "walk"), P("groups", None, "walk")),
        check_vma=False,
    )
```

```python
import functools

import jax
import jax.numpy as jnp
from jax import lax
from jax.experimental import pallas as pl
from jax.experimental.pallas import tpu as pltpu
from jax.sharding import PartitionSpec as P

TERMS = 6


root_step = 0.05
highest = lax.Precision.HIGHEST
LANES = 128
SUB = LANES // 2
SUBS = 3
f32 = jnp.float32
bf16 = jnp.bfloat16


def swapped(value, axis, apart):
    mask = 2**apart
    pairs = [(source, source ^ mask) for source in range(lax.axis_size(axis))]
    return lax.ppermute(value, axis, pairs)


def solve_normal(factor, right_side):
    middle = lax.linalg.triangular_solve(factor, right_side, left_side=True, lower=True)
    return lax.linalg.triangular_solve(factor, middle, left_side=True, lower=True, transpose_a=True)


def green_blocks(walker_full, trial_orbitals, trial_part, row_groups, col_groups):
    owner_walkers, orbital_count, electron_count = walker_full.shape
    intersection = jnp.einsum("nm,wnk->wmk", trial_orbitals, walker_full, precision=highest)
    normal = jnp.einsum("wmk,wml->wkl", intersection, intersection, precision=highest)
    factor = jnp.linalg.cholesky(normal)
    rotated = jnp.einsum("wmk,cbm->wkcb", intersection, trial_part, precision=highest)
    chosen_cols = rotated.shape[2] * rotated.shape[3]
    solved = solve_normal(factor, rotated.reshape(owner_walkers, electron_count, chosen_cols))
    slab_rows = orbital_count // row_groups
    block_cols = chosen_cols // col_groups
    shaped = solved.reshape(owner_walkers, electron_count, col_groups, block_cols)
    walker_rows = walker_full.reshape(owner_walkers, row_groups, slab_rows, electron_count)
    blocks = jnp.einsum("wiak,wkcb->icwab", walker_rows, shaped, precision=highest)
    return blocks.astype(jnp.bfloat16).reshape(
        row_groups * col_groups, owner_walkers, slab_rows * block_cols
    )


def shards(chol_vectors, trial_orbitals, walkers, field_noise):
    held_vectors, slab_rows, slab_cols = chol_vectors.shape
    owner_walkers = walkers.shape[0]
    orbital_count = walkers.shape[1]
    electron_count = trial_orbitals.shape[1]
    row_groups = lax.axis_size("pairs")
    col_groups = lax.axis_size("chol")
    core_count = lax.axis_size("walk")
    core_index = lax.axis_index("walk")
    core_cols = slab_cols // core_count
    owner_count = row_groups * col_groups
    walker_total = owner_count * owner_walkers
    flat_vectors = chol_vectors.reshape(held_vectors, slab_rows * slab_cols)
    trial_split = trial_orbitals.reshape(col_groups, core_count, core_cols, electron_count)
    trial_part = lax.dynamic_index_in_dim(trial_split, core_index, 1, keepdims=False)
    walker_full = lax.all_gather(walkers, "walk", axis=2, tiled=True)
    outgoing = green_blocks(walker_full, trial_orbitals, trial_part, row_groups, col_groups)
    sectioned = outgoing.reshape(row_groups, col_groups, owner_walkers, slab_rows * core_cols)
    arrived = lax.all_to_all(
        lax.all_to_all(sectioned, "pairs", split_axis=0, concat_axis=0, tiled=True),
        "chol",
        split_axis=1,
        concat_axis=1,
        tiled=True,
    )
    arrived = arrived.reshape(walker_total, slab_rows, core_cols)
    partial_bias = jnp.einsum(
        "wab,gab->wg",
        lax.all_gather(arrived, "walk", axis=2, tiled=True),
        chol_vectors,
        preferred_element_type=jnp.float32,
    )
    force_bias = lax.psum(partial_bias, ("pairs", "chol"))
    bias_steps = [force_bias]
    shifted = field_noise[0] + root_step * force_bias
    shifted_high = lax.optimization_barrier(shifted.astype(jnp.bfloat16))
    shifted_low = (shifted - shifted_high.astype(jnp.float32)).astype(jnp.bfloat16)
    stacked = jnp.stack([shifted_high, shifted_low])
    both_parts = lax.dot_general(
        stacked, flat_vectors, (((2,), (0,)), ((), ())), preferred_element_type=jnp.float32
    )
    potential = both_parts[0] + both_parts[1]
    blocks_out = potential.reshape(owner_count, owner_walkers, slab_rows * slab_cols)
    received = lax.all_to_all(
        blocks_out, ("pairs", "chol"), split_axis=0, concat_axis=0, tiled=True
    )
    partner = swapped(received, "walk", 0)
    summed = (received + partner).reshape(
        row_groups, col_groups, owner_walkers, slab_rows, core_count, core_cols
    )
    matrix = jnp.transpose(summed, (2, 0, 3, 1, 4, 5)).reshape(
        owner_walkers, orbital_count, orbital_count
    )
    running_term = walkers
    running_sum = walkers
    for degree in range(1, TERMS):
        running_term = -(root_step / degree) * jnp.einsum(
            "wpq,wqm->wpm", matrix, running_term, precision=highest
        )
        running_sum = running_sum + running_term
    return (running_sum, jnp.stack(bias_steps))


def split_two(value):
    high = value.astype(bf16)
    return high, (value - high.astype(f32)).astype(bf16)


def dot_of(left, right, dims=(((1,), (0,)), ((), ())), precision=None):
    return lax.dot_general(left, right, dims, precision=precision, preferred_element_type=f32)


def dot_three(left, right, dims=(((1,), (0,)), ((), ()))):
    left_high, left_low = split_two(left)
    right_high, right_low = split_two(right)
    return (
        dot_of(left_high, right_high, dims)
        + dot_of(left_high, right_low, dims)
        + dot_of(left_low, right_high, dims)
    )


first_dims = (((0,), (0,)), ((), ()))
last_dims = (((1,), (1,)), ((), ()))


def eye_of(size):
    rows = lax.broadcasted_iota(jnp.int32, (size, size), 0)
    cols = lax.broadcasted_iota(jnp.int32, (size, size), 1)
    return (rows == cols).astype(f32)


def half_rolled(value):
    return pltpu.roll(value, LANES // 2, 1)


def tail_lanes(value):
    return lax.broadcasted_iota(jnp.int32, value.shape, 1) < LANES // 2


LOW_START = 5e-4
PAIRED_STEPS = 6
RESIDUAL_BOUND = 3e-3
MOST_STEPS = 60


def scales():
    low = LOW_START
    found = []
    for _ in range(PAIRED_STEPS + 1):
        scale = 2.0 / (1.0 + 2.0 * low - low * low)
        found.append(scale)
        low = 2.0 - scale
    return found


def green_body(core_ref, own_ref, other_ref, trial_ref, out_ref, inverse_ref, matrix_ref, solved_ref, *, row_groups, col_groups):
    orbital_count, electron_count = trial_ref.shape
    slab_rows = orbital_count // row_groups
    slab_cols = orbital_count // col_groups
    core = core_ref[0]
    walker = jnp.concatenate([own_ref[...], other_ref[...]], axis=1)
    trial = trial_ref[...]
    inter = dot_of(trial, walker, first_dims, highest)
    inverse_scale = 1.0 / jnp.max(jnp.abs(inter))
    inter = inter * inverse_scale
    matrix_ref[...] = inter
    turned = inter.T
    eye = eye_of(electron_count)
    normal = dot_three(turned, inter)
    both = dot_three(normal, jnp.concatenate([normal, turned], axis=1))
    square = both[:, :electron_count]
    step_scales = scales()
    largest = jnp.sqrt(jnp.sqrt(jnp.sum(square * square))) * 1.001
    alpha = (2.0 - LOW_START) / largest
    scale = step_scales[0]
    error = eye - (2.0 * scale * alpha) * normal + (scale * alpha * alpha) * square
    inverse = (scale * alpha) * (2.0 * turned - alpha * both[:, electron_count:])
    for scale in step_scales[1:]:
        both = dot_three(error, jnp.concatenate([error, inverse], axis=1))
        inverse = scale * (inverse + both[:, electron_count:])
        error = (1.0 - scale) * eye + scale * both[:, :electron_count]
    inverse_ref[...] = inverse

    def refine(carried):
        count, _ = carried
        current = inverse_ref[...]
        residual = eye_of(electron_count) - dot_of(current, matrix_ref[...], precision=highest)
        inverse_ref[...] = current + dot_three(residual, current)
        return count + 1, jnp.sum(residual * residual)

    lax.while_loop(
        lambda carried: jnp.logical_and(carried[0] < MOST_STEPS, carried[1] > RESIDUAL_BOUND**2),
        refine,
        (jnp.int32(0), jnp.float32(1e30)),
    )
    walker_rows = dot_three(
        jnp.concatenate([own_ref[...], other_ref[...]], axis=1), inverse_ref[...]
    )
    solved_ref[...] = walker_rows * inverse_scale
    part = SUB // 2
    empty = jnp.zeros((SUB, electron_count), f32)
    for sub in range(SUBS):
        following = (sub + 1) % SUBS
        starts = [
            pl.multiple_of(row * slab_rows + sub * SUB + core * part, 8) for row in range(row_groups)
        ]
        left = jnp.concatenate([solved_ref[pl.ds(start, part), :] for start in starts], axis=0)
        left_turned = jnp.concatenate([trial_ref[pl.ds(start, part), :] for start in starts], axis=0)
        right = []
        right_turned = []
        for col in range(col_groups):
            same = col * slab_cols + sub * SUB
            next_one = col * slab_cols + following * SUB
            right += [trial_ref[same : same + SUB, :], trial_ref[next_one : next_one + SUB, :]]
            right_turned += [empty, solved_ref[next_one : next_one + SUB, :]]
        green = dot_three(left, jnp.concatenate(right, axis=0), last_dims)
        turned = dot_three(left_turned, jnp.concatenate(right_turned, axis=0), last_dims)
        summed = green.astype(bf16).astype(f32) + turned.astype(bf16).astype(f32)
        summed = summed.astype(bf16)
        for row in range(row_groups):
            for col in range(col_groups):
                out_ref[row * col_groups + col, sub * part : (sub + 1) * part, :] = summed[
                    row * part : (row + 1) * part, col * LANES : (col + 1) * LANES
                ]


def bias_body(place_ref, green_ref, same_ref, next_ref, before_ref, out_ref, turned_ref, total_ref):
    step = pl.program_id(0)
    block = same_ref.shape[0]

    @pl.when(step == 0)
    def _():
        turned_ref[...] = jnp.swapaxes(green_ref[...].astype(f32), 0, 1).astype(bf16)
        total_ref[...] = before_ref[...]

    left = [turned_ref[step * block + row] for row in range(block)]
    right = []
    for row in range(block):
        right += [same_ref[row], next_ref[row]]
    total = dot_of(jnp.concatenate(left, axis=1), jnp.concatenate(right, axis=0))
    total_ref[...] = total_ref[...] + total

    @pl.when(step == pl.num_programs(0) - 1)
    def _():
        for device in range(out_ref.shape[0]):
            out_ref[device] = total_ref[...]


def potential_body(place_ref, parts_ref, noise_ref, same_ref, next_ref, bias_ref, out_ref, weights_ref):
    step = pl.program_id(0)
    walker_total = noise_ref.shape[0]
    block = same_ref.shape[0]

    @pl.when(step == 0)
    def _():
        bias = parts_ref[0]
        for device in range(1, parts_ref.shape[0]):
            bias = bias + parts_ref[device]
        bias_ref[...] = bias
        high, low = split_two(noise_ref[...] + root_step * bias)
        weights_ref[...] = jnp.concatenate([high, low], axis=0)

    right = []
    for row in range(block):
        right += [same_ref[row], next_ref[row]]
    both = dot_of(weights_ref[...], jnp.concatenate(right, axis=0), last_dims)
    added = both[:walker_total] + both[walker_total:]
    for row in range(block):
        out_ref[step * block + row] = added[:, row * LANES : (row + 1) * LANES]


def series_body(core_ref, own_ref, other_ref, walker_ref, out_ref, matrix_ref, *, row_groups, col_groups):
    slab = SUB * SUBS
    part = SUB // 2
    size = row_groups * SUB
    core = core_ref[0]
    for source, place in ((own_ref, core), (other_ref, 1 - core)):
        for sub in range(SUBS):
            following = (sub + 1) % SUBS
            for row in range(row_groups):
                start = pl.multiple_of(sub * size + row * SUB + place * part, 16)
                for col in range(0, col_groups, 2):
                    index = row * col_groups + col
                    even = source[index, sub * part : (sub + 1) * part, :].astype(f32)
                    odd = source[index + 1, sub * part : (sub + 1) * part, :].astype(f32)
                    same = jnp.where(tail_lanes(even), even, half_rolled(odd)).astype(bf16)
                    beside = jnp.where(tail_lanes(even), half_rolled(even), odd).astype(bf16)
                    lane = col // 2 * LANES
                    matrix_ref[pl.ds(start, part), sub * size + lane : sub * size + lane + LANES] = same
                    lane += following * size
                    matrix_ref[pl.ds(start, part), lane : lane + LANES] = beside
    for sub in range(SUBS):
        following = (sub + 1) % SUBS
        block = matrix_ref[sub * size : (sub + 1) * size, following * size : (following + 1) * size]
        matrix_ref[following * size : (following + 1) * size, sub * size : (sub + 1) * size] = (
            block.astype(f32).T.astype(bf16)
        )

    pieces = []
    for sub in range(SUBS):
        for row in range(row_groups):
            pieces.append(walker_ref[row * slab + sub * SUB : row * slab + (sub + 1) * SUB, :])
    term = jnp.concatenate(pieces, axis=0)
    total = term
    width = term.shape[1]
    for degree in range(1, TERMS):
        high, low = split_two(term)
        both = dot_of(matrix_ref[...], jnp.concatenate([high, low], axis=1))
        term = (-root_step / degree) * (both[:, :width] + both[:, width:])
        total = total + term
    for sub in range(SUBS):
        for row in range(row_groups):
            start = sub * size + row * SUB
            out_ref[row * slab + sub * SUB : row * slab + (sub + 1) * SUB, :] = total[start : start + SUB]


smem = pl.BlockSpec(memory_space=pltpu.SMEM)
vmem = pl.BlockSpec(memory_space=pltpu.VMEM)
grant = pltpu.CompilerParams(vmem_limit_bytes=16 * 2**20)
large_grant = pltpu.CompilerParams(vmem_limit_bytes=46 * 2**20)


def whole(*shape):
    return pl.BlockSpec(shape, lambda step, place: (0,) * len(shape))


def half_blocks(held, shift):
    return pl.BlockSpec(
        (SUB // 2, SUB, held), lambda step, place: (2 * step + place[0], (step + shift) % SUBS, 0)
    )


def bias_half(place, green, vectors, before, copies):
    owners, dense, _ = green.shape
    held = vectors.shape[2]
    return pl.pallas_call(
        bias_body,
        grid_spec=pltpu.PrefetchScalarGridSpec(
            num_scalar_prefetch=1,
            grid=(SUBS,),
            in_specs=[
                whole(owners, dense, LANES),
                half_blocks(held, 0),
                half_blocks(held, 1),
                whole(owners, held),
            ],
            out_specs=whole(copies, owners, held),
            scratch_shapes=[
                pltpu.VMEM((dense, owners, LANES), bf16),
                pltpu.VMEM((owners, held), f32),
            ],
        ),
        out_shape=jax.ShapeDtypeStruct((copies, owners, held), f32),
        compiler_params=large_grant,
        name="bias",
    )(place, green, vectors, vectors, before)


def potential_half(place, parts, noise, vectors):
    count, owners, held = parts.shape
    dense = SUBS * SUB // 2
    return pl.pallas_call(
        potential_body,
        grid_spec=pltpu.PrefetchScalarGridSpec(
            num_scalar_prefetch=1,
            grid=(SUBS,),
            in_specs=[
                whole(count, owners, held),
                whole(owners, held),
                half_blocks(held, 0),
                half_blocks(held, 1),
            ],
            out_specs=(whole(owners, held), whole(dense, owners, LANES)),
            scratch_shapes=[pltpu.VMEM((2 * owners, held), bf16)],
        ),
        out_shape=(
            jax.ShapeDtypeStruct((owners, held), f32),
            jax.ShapeDtypeStruct((dense, owners, LANES), f32),
        ),
        compiler_params=large_grant,
        name="potential",
    )(place, parts, noise, vectors, vectors)


def fast_shards(chol_vectors, trial_orbitals, walkers, field_noise):
    held = chol_vectors.shape[0]
    orbital_count, electron_count = trial_orbitals.shape
    row_groups = lax.axis_size("pairs")
    col_groups = lax.axis_size("chol")
    owners = row_groups * col_groups
    dense = SUBS * SUB // 2
    core = lax.axis_index("walk").astype(jnp.int32).reshape(1)
    vectors = jnp.transpose(chol_vectors, (1, 2, 0))
    own = walkers[0]
    other = swapped(own, "walk", 0)
    square = pltpu.VMEM((electron_count, electron_count), f32)
    outgoing = pl.pallas_call(
        functools.partial(green_body, row_groups=row_groups, col_groups=col_groups),
        out_shape=jax.ShapeDtypeStruct((owners, dense, LANES), bf16),
        in_specs=[smem, vmem, vmem, vmem],
        out_specs=vmem,
        scratch_shapes=[square, square, pltpu.VMEM((orbital_count, electron_count), f32)],
        compiler_params=grant,
        name="green",
    )(core, own, other, trial_orbitals)
    axes = ("pairs", "chol")
    arrived = lax.all_to_all(outgoing, axes, split_axis=0, concat_axis=0, tiled=True)
    arrived_other = swapped(arrived, "walk", 0)
    first = bias_half(core, arrived, vectors, jnp.zeros((owners, held), f32), 1)
    spread = bias_half(1 - core, arrived_other, vectors, first[0], owners)
    parts = lax.all_to_all(spread, axes, split_axis=0, concat_axis=0, tiled=True)
    force_bias, send = potential_half(1 - core, parts, field_noise[0], vectors)
    _, keep = potential_half(core, parts, field_noise[0], vectors)
    summed = jnp.swapaxes((keep + swapped(send, "walk", 0)).astype(bf16), 0, 1)
    received = lax.all_to_all(summed, axes, split_axis=0, concat_axis=0, tiled=True)
    received_other = swapped(received, "walk", 0)
    propagated = pl.pallas_call(
        functools.partial(series_body, row_groups=row_groups, col_groups=col_groups),
        out_shape=jax.ShapeDtypeStruct(own.shape, f32),
        in_specs=[smem, vmem, vmem, vmem],
        out_specs=vmem,
        scratch_shapes=[pltpu.VMEM((orbital_count, orbital_count), bf16)],
        compiler_params=grant,
        name="series",
    )(core, received, received_other, own)
    return propagated[None], force_bias[None]


def packable(chol_vectors, trial_orbitals, walkers, field_noise):
    held, slab_rows, slab_cols = chol_vectors.shape
    row_groups = lax.axis_size("pairs")
    return (
        walkers.shape[0] == 1
        and lax.axis_size("walk") == 2
        and lax.axis_size("chol") == row_groups
        and row_groups in (2, 4, 8)
        and slab_cols == slab_rows == SUB * SUBS
        and held % LANES == 0
        and trial_orbitals.shape[1] % LANES == 0
        and field_noise.shape[0] == 1
    )


def chosen_shards(*args):
    return fast_shards(*args) if packable(*args) else shards(*args)


def solution(mesh):
    placed = (
        P(("groups", "walk"), "pairs", "chol"),
        P("groups", None),
        P(("groups", "pairs", "chol"), None, "walk"),
        P("groups", None, "walk"),
    )
    return jax.shard_map(
        chosen_shards,
        mesh=mesh,
        in_specs=placed,
        out_specs=(P(("groups", "pairs", "chol"), None, "walk"), P("groups", None, "walk")),
        check_vma=False,
    )
```

```python
import functools

import jax
import jax.numpy as jnp
from jax import lax
from jax.experimental import pallas as pl
from jax.experimental.pallas import tpu as pltpu
from jax.sharding import PartitionSpec as P

TERMS = 6


root_step = 0.05
highest = lax.Precision.HIGHEST
LANES = 128
SUB = LANES // 2
SUBS = 3
f32 = jnp.float32
bf16 = jnp.bfloat16


def swapped(value, axis, apart):
    mask = 2**apart
    pairs = [(source, source ^ mask) for source in range(lax.axis_size(axis))]
    return lax.ppermute(value, axis, pairs)


def solve_normal(factor, right_side):
    middle = lax.linalg.triangular_solve(factor, right_side, left_side=True, lower=True)
    return lax.linalg.triangular_solve(factor, middle, left_side=True, lower=True, transpose_a=True)


def green_blocks(walker_full, trial_orbitals, trial_part, row_groups, col_groups):
    owner_walkers, orbital_count, electron_count = walker_full.shape
    intersection = jnp.einsum("nm,wnk->wmk", trial_orbitals, walker_full, precision=highest)
    normal = jnp.einsum("wmk,wml->wkl", intersection, intersection, precision=highest)
    factor = jnp.linalg.cholesky(normal)
    rotated = jnp.einsum("wmk,cbm->wkcb", intersection, trial_part, precision=highest)
    chosen_cols = rotated.shape[2] * rotated.shape[3]
    solved = solve_normal(factor, rotated.reshape(owner_walkers, electron_count, chosen_cols))
    slab_rows = orbital_count // row_groups
    block_cols = chosen_cols // col_groups
    shaped = solved.reshape(owner_walkers, electron_count, col_groups, block_cols)
    walker_rows = walker_full.reshape(owner_walkers, row_groups, slab_rows, electron_count)
    blocks = jnp.einsum("wiak,wkcb->icwab", walker_rows, shaped, precision=highest)
    return blocks.astype(jnp.bfloat16).reshape(
        row_groups * col_groups, owner_walkers, slab_rows * block_cols
    )


def shards(chol_vectors, trial_orbitals, walkers, field_noise):
    held_vectors, slab_rows, slab_cols = chol_vectors.shape
    owner_walkers = walkers.shape[0]
    orbital_count = walkers.shape[1]
    electron_count = trial_orbitals.shape[1]
    row_groups = lax.axis_size("pairs")
    col_groups = lax.axis_size("chol")
    core_count = lax.axis_size("walk")
    core_index = lax.axis_index("walk")
    core_cols = slab_cols // core_count
    owner_count = row_groups * col_groups
    walker_total = owner_count * owner_walkers
    flat_vectors = chol_vectors.reshape(held_vectors, slab_rows * slab_cols)
    trial_split = trial_orbitals.reshape(col_groups, core_count, core_cols, electron_count)
    trial_part = lax.dynamic_index_in_dim(trial_split, core_index, 1, keepdims=False)
    walker_full = lax.all_gather(walkers, "walk", axis=2, tiled=True)
    outgoing = green_blocks(walker_full, trial_orbitals, trial_part, row_groups, col_groups)
    sectioned = outgoing.reshape(row_groups, col_groups, owner_walkers, slab_rows * core_cols)
    arrived = lax.all_to_all(
        lax.all_to_all(sectioned, "pairs", split_axis=0, concat_axis=0, tiled=True),
        "chol",
        split_axis=1,
        concat_axis=1,
        tiled=True,
    )
    arrived = arrived.reshape(walker_total, slab_rows, core_cols)
    partial_bias = jnp.einsum(
        "wab,gab->wg",
        lax.all_gather(arrived, "walk", axis=2, tiled=True),
        chol_vectors,
        preferred_element_type=jnp.float32,
    )
    force_bias = lax.psum(partial_bias, ("pairs", "chol"))
    bias_steps = [force_bias]
    shifted = field_noise[0] + root_step * force_bias
    shifted_high = lax.optimization_barrier(shifted.astype(jnp.bfloat16))
    shifted_low = (shifted - shifted_high.astype(jnp.float32)).astype(jnp.bfloat16)
    stacked = jnp.stack([shifted_high, shifted_low])
    both_parts = lax.dot_general(
        stacked, flat_vectors, (((2,), (0,)), ((), ())), preferred_element_type=jnp.float32
    )
    potential = both_parts[0] + both_parts[1]
    blocks_out = potential.reshape(owner_count, owner_walkers, slab_rows * slab_cols)
    received = lax.all_to_all(
        blocks_out, ("pairs", "chol"), split_axis=0, concat_axis=0, tiled=True
    )
    partner = swapped(received, "walk", 0)
    summed = (received + partner).reshape(
        row_groups, col_groups, owner_walkers, slab_rows, core_count, core_cols
    )
    matrix = jnp.transpose(summed, (2, 0, 3, 1, 4, 5)).reshape(
        owner_walkers, orbital_count, orbital_count
    )
    running_term = walkers
    running_sum = walkers
    for degree in range(1, TERMS):
        running_term = -(root_step / degree) * jnp.einsum(
            "wpq,wqm->wpm", matrix, running_term, precision=highest
        )
        running_sum = running_sum + running_term
    return (running_sum, jnp.stack(bias_steps))


def split_two(value):
    high = value.astype(bf16)
    return high, (value - high.astype(f32)).astype(bf16)


def dot_of(left, right, dims=(((1,), (0,)), ((), ())), precision=None):
    return lax.dot_general(left, right, dims, precision=precision, preferred_element_type=f32)


def dot_three(left, right, dims=(((1,), (0,)), ((), ()))):
    left_high, left_low = split_two(left)
    right_high, right_low = split_two(right)
    return (
        dot_of(left_high, right_high, dims)
        + dot_of(left_high, right_low, dims)
        + dot_of(left_low, right_high, dims)
    )


first_dims = (((0,), (0,)), ((), ()))
last_dims = (((1,), (1,)), ((), ()))


def eye_of(size):
    rows = lax.broadcasted_iota(jnp.int32, (size, size), 0)
    cols = lax.broadcasted_iota(jnp.int32, (size, size), 1)
    return (rows == cols).astype(f32)


def half_rolled(value):
    return pltpu.roll(value, LANES // 2, 1)


def tail_lanes(value):
    return lax.broadcasted_iota(jnp.int32, value.shape, 1) < LANES // 2


LOW_START = 5e-4
PAIRED_STEPS = 8
RESIDUAL_BOUND = 1e-2
MOST_STEPS = 60


def scales():
    low = LOW_START
    found = []
    for _ in range(PAIRED_STEPS + 1):
        scale = 2.0 / (1.0 + 2.0 * low - low * low)
        found.append(scale)
        low = 2.0 - scale
    return found


def overlap_body(own_ref, trial_ref, inter_ref, turned_ref):
    turned_ref[...] = trial_ref[...].T
    inter_ref[...] = dot_of(turned_ref[...], own_ref[...], precision=highest)


def green_body(
    core_ref, other_ref, inter_ref, trial_turned_ref, own_hbm_ref, trial_hbm_ref, vector_ref,
    out_ref, kept_ref, inverse_ref, matrix_ref, solved_ref, own_ref, trial_ref, sems,
    *, row_groups, col_groups
):
    early = [
        pltpu.make_async_copy(own_hbm_ref, own_ref, sems.at[2 * SUBS]),
        pltpu.make_async_copy(trial_hbm_ref, trial_ref, sems.at[2 * SUBS + 1]),
    ]
    for copy in early:
        copy.start()
    copies = []
    for sub in range(SUBS):
        rows = pl.ds(sub * SUB, SUB)
        for beside in range(2):
            cols = pl.ds((sub + beside) % SUBS * SUB, SUB)
            copies.append(
                pltpu.make_async_copy(
                    vector_ref.at[rows, cols, :],
                    kept_ref.at[rows, pl.ds(beside * SUB, SUB), :],
                    sems.at[2 * sub + beside],
                )
            )
            copies[-1].start()
    orbital_count, electron_count = trial_ref.shape
    slab_rows = orbital_count // row_groups
    slab_cols = orbital_count // col_groups
    core = core_ref[0]
    inter_other = dot_of(trial_turned_ref[...], other_ref[...], precision=highest)
    inter = jnp.concatenate([inter_ref[...], inter_other], axis=1)
    inverse_scale = 1.0 / jnp.max(jnp.abs(inter))
    inter = inter * inverse_scale
    matrix_ref[...] = inter
    turned = inter.T
    eye = eye_of(electron_count)
    normal = dot_three(turned, inter)
    both = dot_three(normal, jnp.concatenate([normal, turned], axis=1))
    square = both[:, :electron_count]
    step_scales = scales()
    largest = jnp.sqrt(jnp.sqrt(jnp.sum(square * square))) * 1.001
    alpha = (2.0 - LOW_START) / largest
    scale = step_scales[0]
    error = eye - (2.0 * scale * alpha) * normal + (scale * alpha * alpha) * square
    inverse = (scale * alpha) * (2.0 * turned - alpha * both[:, electron_count:])
    for scale in step_scales[1:-1]:
        both = dot_three(error, jnp.concatenate([error, inverse], axis=1))
        inverse = scale * (inverse + both[:, electron_count:])
        error = (1.0 - scale) * eye + scale * both[:, :electron_count]
    inverse = step_scales[-1] * (inverse + dot_three(error, inverse))
    inverse_ref[...] = inverse

    def refine(carried):
        count, _ = carried
        current = inverse_ref[...]
        residual = eye_of(electron_count) - dot_of(current, matrix_ref[...], precision=highest)
        inverse_ref[...] = current + dot_three(residual, current)
        return count + 1, jnp.sum(residual * residual)

    lax.while_loop(
        lambda carried: jnp.logical_and(carried[0] < MOST_STEPS, carried[1] > RESIDUAL_BOUND**2),
        refine,
        (jnp.int32(0), jnp.float32(1e30)),
    )
    for copy in early:
        copy.wait()
    walker_rows = dot_three(
        jnp.concatenate([own_ref[...], other_ref[...]], axis=1), inverse_ref[...]
    )
    solved_ref[...] = walker_rows * inverse_scale
    part = SUB // 2
    empty = jnp.zeros((SUB, electron_count), f32)
    for sub in range(SUBS):
        following = (sub + 1) % SUBS
        starts = [
            pl.multiple_of(row * slab_rows + sub * SUB + core * part, 8) for row in range(row_groups)
        ]
        left = jnp.concatenate([solved_ref[pl.ds(start, part), :] for start in starts], axis=0)
        left_turned = jnp.concatenate([trial_ref[pl.ds(start, part), :] for start in starts], axis=0)
        right = []
        right_turned = []
        for col in range(col_groups):
            same = col * slab_cols + sub * SUB
            next_one = col * slab_cols + following * SUB
            right += [trial_ref[same : same + SUB, :], trial_ref[next_one : next_one + SUB, :]]
            right_turned += [empty, solved_ref[next_one : next_one + SUB, :]]
        green = dot_three(left, jnp.concatenate(right, axis=0), last_dims)
        turned = dot_three(left_turned, jnp.concatenate(right_turned, axis=0), last_dims)
        summed = green.astype(bf16).astype(f32) + turned.astype(bf16).astype(f32)
        summed = summed.astype(bf16)
        for row in range(row_groups):
            for col in range(col_groups):
                out_ref[row * col_groups + col, sub * part : (sub + 1) * part, :] = summed[
                    row * part : (row + 1) * part, col * LANES : (col + 1) * LANES
                ]
    for copy in copies:
        copy.wait()


def kept_rows(kept_ref, sub, place):
    part = SUB // 2
    start = pl.multiple_of(sub * SUB + place * part, part)
    return kept_ref[pl.ds(start, part)].reshape(part * LANES, kept_ref.shape[2])


def bias_body(place_ref, green_ref, kept_ref, before_ref, out_ref, turned_ref):
    part = SUB // 2
    place = place_ref[0]
    turned_ref[...] = jnp.swapaxes(green_ref[...].astype(f32), 0, 1).astype(bf16)
    total = before_ref[...]
    for sub in range(SUBS):
        left = [turned_ref[sub * part + row] for row in range(part)]
        total = total + dot_of(jnp.concatenate(left, axis=1), kept_rows(kept_ref, sub, place))
    for device in range(out_ref.shape[0]):
        out_ref[device] = total


def potential_body(place_ref, parts_ref, noise_ref, kept_ref, bias_ref, out_ref):
    part = SUB // 2
    place = place_ref[0]
    walker_total = noise_ref.shape[0]
    bias = parts_ref[0]
    for device in range(1, parts_ref.shape[0]):
        bias = bias + parts_ref[device]
    bias_ref[...] = bias
    high, low = split_two(noise_ref[...] + root_step * bias)
    weights = jnp.concatenate([high, low], axis=0)
    for sub in range(SUBS):
        both = dot_of(weights, kept_rows(kept_ref, sub, place), last_dims)
        added = both[:walker_total] + both[walker_total:]
        for row in range(part):
            out_ref[sub * part + row] = added[:, row * LANES : (row + 1) * LANES]


def series_body(core_ref, own_ref, other_ref, walker_ref, out_ref, matrix_ref, *, row_groups, col_groups):
    slab = SUB * SUBS
    part = SUB // 2
    size = row_groups * SUB
    core = core_ref[0]
    for source, place in ((own_ref, core), (other_ref, 1 - core)):
        for sub in range(SUBS):
            following = (sub + 1) % SUBS
            for row in range(row_groups):
                start = pl.multiple_of(sub * size + row * SUB + place * part, 16)
                for col in range(0, col_groups, 2):
                    index = row * col_groups + col
                    even = source[index, sub * part : (sub + 1) * part, :].astype(f32)
                    odd = source[index + 1, sub * part : (sub + 1) * part, :].astype(f32)
                    same = jnp.where(tail_lanes(even), even, half_rolled(odd)).astype(bf16)
                    beside = jnp.where(tail_lanes(even), half_rolled(even), odd).astype(bf16)
                    lane = col // 2 * LANES
                    matrix_ref[pl.ds(start, part), sub * size + lane : sub * size + lane + LANES] = same
                    lane += following * size
                    matrix_ref[pl.ds(start, part), lane : lane + LANES] = beside
    for sub in range(SUBS):
        following = (sub + 1) % SUBS
        block = matrix_ref[sub * size : (sub + 1) * size, following * size : (following + 1) * size]
        matrix_ref[following * size : (following + 1) * size, sub * size : (sub + 1) * size] = (
            block.astype(f32).T.astype(bf16)
        )

    pieces = []
    for sub in range(SUBS):
        for row in range(row_groups):
            pieces.append(walker_ref[row * slab + sub * SUB : row * slab + (sub + 1) * SUB, :])
    term = jnp.concatenate(pieces, axis=0)
    total = term
    width = term.shape[1]
    for degree in range(1, TERMS):
        high, low = split_two(term)
        both = dot_of(matrix_ref[...], jnp.concatenate([high, low], axis=1))
        term = (-root_step / degree) * (both[:, :width] + both[:, width:])
        total = total + term
    for sub in range(SUBS):
        for row in range(row_groups):
            start = sub * size + row * SUB
            out_ref[row * slab + sub * SUB : row * slab + (sub + 1) * SUB, :] = total[start : start + SUB]


smem = pl.BlockSpec(memory_space=pltpu.SMEM)
vmem = pl.BlockSpec(memory_space=pltpu.VMEM)
anywhere = pl.BlockSpec(memory_space=pl.ANY)
grant = pltpu.CompilerParams(vmem_limit_bytes=20 * 2**20)


def bias_half(place, green, kept, before, copies):
    owners, dense, _ = green.shape
    held = kept.shape[2]
    return pl.pallas_call(
        bias_body,
        in_specs=[smem, vmem, vmem, vmem],
        out_specs=vmem,
        scratch_shapes=[pltpu.VMEM((dense, owners, LANES), bf16)],
        out_shape=jax.ShapeDtypeStruct((copies, owners, held), f32),
        compiler_params=grant,
        name="bias",
    )(place, green, in_vmem(kept), before)


def in_hbm(value):
    return pltpu.with_memory_space_constraint(value, pltpu.HBM)


def in_vmem(value):
    return pltpu.with_memory_space_constraint(value, pltpu.VMEM)


def potential_half(place, parts, noise, kept):
    _, owners, held = parts.shape
    return pl.pallas_call(
        potential_body,
        in_specs=[smem, vmem, vmem, vmem],
        out_specs=(vmem, vmem),
        out_shape=(
            jax.ShapeDtypeStruct((owners, held), f32),
            jax.ShapeDtypeStruct((SUBS * SUB // 2, owners, LANES), f32),
        ),
        compiler_params=grant,
        name="potential",
    )(place, parts, noise, in_vmem(kept))


def fast_shards(chol_vectors, trial_orbitals, walkers, field_noise):
    held = chol_vectors.shape[0]
    orbital_count, electron_count = trial_orbitals.shape
    row_groups = lax.axis_size("pairs")
    col_groups = lax.axis_size("chol")
    owners = row_groups * col_groups
    dense = SUBS * SUB // 2
    core = lax.axis_index("walk").astype(jnp.int32).reshape(1)
    vectors = jnp.transpose(chol_vectors, (1, 2, 0))
    own = walkers[0]
    other = swapped(own, "walk", 0)
    inter, trial_turned = pl.pallas_call(
        overlap_body,
        out_shape=(
            jax.ShapeDtypeStruct((electron_count, own.shape[1]), f32),
            jax.ShapeDtypeStruct((electron_count, orbital_count), f32),
        ),
        in_specs=[vmem, vmem],
        out_specs=(vmem, vmem),
        compiler_params=grant,
        name="overlap",
    )(in_hbm(own), in_hbm(trial_orbitals))
    square = pltpu.VMEM((electron_count, electron_count), f32)
    outgoing, kept = pl.pallas_call(
        functools.partial(green_body, row_groups=row_groups, col_groups=col_groups),
        out_shape=(
            jax.ShapeDtypeStruct((owners, dense, LANES), bf16),
            pltpu.VMEM((SUBS * SUB, LANES, held), bf16),
        ),
        in_specs=[smem, vmem, vmem, vmem, anywhere, anywhere, anywhere],
        out_specs=(vmem, vmem),
        scratch_shapes=[
            square,
            square,
            pltpu.VMEM((orbital_count, electron_count), f32),
            pltpu.VMEM(own.shape, f32),
            pltpu.VMEM(trial_orbitals.shape, f32),
            pltpu.SemaphoreType.DMA((2 * SUBS + 2,)),
        ],
        compiler_params=grant,
        name="green",
    )(core, other, inter, trial_turned, in_hbm(own), in_hbm(trial_orbitals), in_hbm(vectors))
    axes = ("pairs", "chol")
    arrived = lax.all_to_all(outgoing, axes, split_axis=0, concat_axis=0, tiled=True)
    arrived_other = swapped(arrived, "walk", 0)
    first = bias_half(core, arrived, kept, jnp.zeros((owners, held), f32), 1)
    spread = bias_half(1 - core, arrived_other, kept, first[0], owners)
    parts = lax.all_to_all(spread, axes, split_axis=0, concat_axis=0, tiled=True)
    force_bias, send = potential_half(1 - core, parts, field_noise[0], kept)
    _, keep = potential_half(core, parts, field_noise[0], kept)
    summed = jnp.swapaxes((keep + swapped(send, "walk", 0)).astype(bf16), 0, 1)
    received = lax.all_to_all(summed, axes, split_axis=0, concat_axis=0, tiled=True)
    received_other = swapped(received, "walk", 0)
    propagated = pl.pallas_call(
        functools.partial(series_body, row_groups=row_groups, col_groups=col_groups),
        out_shape=jax.ShapeDtypeStruct(own.shape, f32),
        in_specs=[smem, vmem, vmem, vmem],
        out_specs=vmem,
        scratch_shapes=[pltpu.VMEM((orbital_count, orbital_count), bf16)],
        compiler_params=grant,
        name="series",
    )(core, received, received_other, own)
    return propagated[None], force_bias[None]


def packable(chol_vectors, trial_orbitals, walkers, field_noise):
    held, slab_rows, slab_cols = chol_vectors.shape
    row_groups = lax.axis_size("pairs")
    return (
        walkers.shape[0] == 1
        and lax.axis_size("walk") == 2
        and lax.axis_size("chol") == row_groups
        and row_groups in (2, 4, 8)
        and slab_cols == slab_rows == SUB * SUBS
        and held % LANES == 0
        and trial_orbitals.shape[1] % LANES == 0
        and field_noise.shape[0] == 1
    )


def chosen_shards(*args):
    return fast_shards(*args) if packable(*args) else shards(*args)


def solution(mesh):
    placed = (
        P(("groups", "walk"), "pairs", "chol"),
        P("groups", None),
        P(("groups", "pairs", "chol"), None, "walk"),
        P("groups", None, "walk"),
    )
    return jax.shard_map(
        chosen_shards,
        mesh=mesh,
        in_specs=placed,
        out_specs=(P(("groups", "pairs", "chol"), None, "walk"), P("groups", None, "walk")),
        check_vma=False,
    )
```

```python
import functools

import jax
import jax.numpy as jnp
from jax import lax
from jax.experimental import pallas as pl
from jax.experimental.pallas import tpu as pltpu
from jax.sharding import PartitionSpec as P

TERMS = 6


root_step = 0.05
highest = lax.Precision.HIGHEST
LANES = 128
SUB = LANES // 2
SUBS = 3
f32 = jnp.float32
bf16 = jnp.bfloat16


def swapped(value, axis, apart):
    mask = 2**apart
    pairs = [(source, source ^ mask) for source in range(lax.axis_size(axis))]
    return lax.ppermute(value, axis, pairs)


def solve_normal(factor, right_side):
    middle = lax.linalg.triangular_solve(factor, right_side, left_side=True, lower=True)
    return lax.linalg.triangular_solve(factor, middle, left_side=True, lower=True, transpose_a=True)


def green_blocks(walker_full, trial_orbitals, trial_part, row_groups, col_groups):
    owner_walkers, orbital_count, electron_count = walker_full.shape
    intersection = jnp.einsum("nm,wnk->wmk", trial_orbitals, walker_full, precision=highest)
    normal = jnp.einsum("wmk,wml->wkl", intersection, intersection, precision=highest)
    factor = jnp.linalg.cholesky(normal)
    rotated = jnp.einsum("wmk,cbm->wkcb", intersection, trial_part, precision=highest)
    chosen_cols = rotated.shape[2] * rotated.shape[3]
    solved = solve_normal(factor, rotated.reshape(owner_walkers, electron_count, chosen_cols))
    slab_rows = orbital_count // row_groups
    block_cols = chosen_cols // col_groups
    shaped = solved.reshape(owner_walkers, electron_count, col_groups, block_cols)
    walker_rows = walker_full.reshape(owner_walkers, row_groups, slab_rows, electron_count)
    blocks = jnp.einsum("wiak,wkcb->icwab", walker_rows, shaped, precision=highest)
    return blocks.astype(jnp.bfloat16).reshape(
        row_groups * col_groups, owner_walkers, slab_rows * block_cols
    )


def shards(chol_vectors, trial_orbitals, walkers, field_noise):
    held_vectors, slab_rows, slab_cols = chol_vectors.shape
    owner_walkers = walkers.shape[0]
    orbital_count = walkers.shape[1]
    electron_count = trial_orbitals.shape[1]
    row_groups = lax.axis_size("pairs")
    col_groups = lax.axis_size("chol")
    core_count = lax.axis_size("walk")
    core_index = lax.axis_index("walk")
    core_cols = slab_cols // core_count
    owner_count = row_groups * col_groups
    walker_total = owner_count * owner_walkers
    flat_vectors = chol_vectors.reshape(held_vectors, slab_rows * slab_cols)
    trial_split = trial_orbitals.reshape(col_groups, core_count, core_cols, electron_count)
    trial_part = lax.dynamic_index_in_dim(trial_split, core_index, 1, keepdims=False)
    walker_full = lax.all_gather(walkers, "walk", axis=2, tiled=True)
    outgoing = green_blocks(walker_full, trial_orbitals, trial_part, row_groups, col_groups)
    sectioned = outgoing.reshape(row_groups, col_groups, owner_walkers, slab_rows * core_cols)
    arrived = lax.all_to_all(
        lax.all_to_all(sectioned, "pairs", split_axis=0, concat_axis=0, tiled=True),
        "chol",
        split_axis=1,
        concat_axis=1,
        tiled=True,
    )
    arrived = arrived.reshape(walker_total, slab_rows, core_cols)
    partial_bias = jnp.einsum(
        "wab,gab->wg",
        lax.all_gather(arrived, "walk", axis=2, tiled=True),
        chol_vectors,
        preferred_element_type=jnp.float32,
    )
    force_bias = lax.psum(partial_bias, ("pairs", "chol"))
    bias_steps = [force_bias]
    shifted = field_noise[0] + root_step * force_bias
    shifted_high = lax.optimization_barrier(shifted.astype(jnp.bfloat16))
    shifted_low = (shifted - shifted_high.astype(jnp.float32)).astype(jnp.bfloat16)
    stacked = jnp.stack([shifted_high, shifted_low])
    both_parts = lax.dot_general(
        stacked, flat_vectors, (((2,), (0,)), ((), ())), preferred_element_type=jnp.float32
    )
    potential = both_parts[0] + both_parts[1]
    blocks_out = potential.reshape(owner_count, owner_walkers, slab_rows * slab_cols)
    received = lax.all_to_all(
        blocks_out, ("pairs", "chol"), split_axis=0, concat_axis=0, tiled=True
    )
    partner = swapped(received, "walk", 0)
    summed = (received + partner).reshape(
        row_groups, col_groups, owner_walkers, slab_rows, core_count, core_cols
    )
    matrix = jnp.transpose(summed, (2, 0, 3, 1, 4, 5)).reshape(
        owner_walkers, orbital_count, orbital_count
    )
    running_term = walkers
    running_sum = walkers
    for degree in range(1, TERMS):
        running_term = -(root_step / degree) * jnp.einsum(
            "wpq,wqm->wpm", matrix, running_term, precision=highest
        )
        running_sum = running_sum + running_term
    return (running_sum, jnp.stack(bias_steps))


def split_two(value):
    high = value.astype(bf16)
    return high, (value - high.astype(f32)).astype(bf16)


def dot_of(left, right, dims=(((1,), (0,)), ((), ())), precision=None):
    return lax.dot_general(left, right, dims, precision=precision, preferred_element_type=f32)


def dot_three(left, right):
    left_high, left_low = split_two(left)
    right_high, right_low = split_two(right)
    return dot_of(
        jnp.concatenate([left_high, left_low, left_high], axis=1),
        jnp.concatenate([right_high, right_high, right_low], axis=0),
    )


first_dims = (((0,), (0,)), ((), ()))
last_dims = (((1,), (1,)), ((), ()))


def eye_of(size):
    rows = lax.broadcasted_iota(jnp.int32, (size, size), 0)
    cols = lax.broadcasted_iota(jnp.int32, (size, size), 1)
    return (rows == cols).astype(f32)


def half_rolled(value):
    return pltpu.roll(value, LANES // 2, 1)


def tail_lanes(value):
    return lax.broadcasted_iota(jnp.int32, value.shape, 1) < LANES // 2


LOW_START = 5e-4
PAIRED_STEPS = 8
RESIDUAL_BOUND = 1e-2
MOST_STEPS = 60


def scales():
    low = LOW_START
    found = []
    for _ in range(PAIRED_STEPS + 1):
        scale = 2.0 / (1.0 + 2.0 * low - low * low)
        found.append(scale)
        low = 2.0 - scale
    return found


def three_terms(left, right, dims=(((1,), (0,)), ((), ()))):
    count = left[0].shape[0]
    both = dot_of(jnp.concatenate(left, axis=0), right[0], dims)
    return both[:count] + both[count:] + dot_of(left[0], right[1], dims)


def overlap_body(own_ref, trial_ref, inter_ref, turned_high_ref, turned_low_ref, high_ref, low_ref, own_high_ref, own_low_ref):
    trial = trial_ref[...]
    own = split_two(own_ref[...])
    turned = split_two(trial.T)
    inter_ref[...] = three_terms(turned, own)
    turned_high_ref[...], turned_low_ref[...] = turned
    high_ref[...], low_ref[...] = split_two(trial)
    own_high_ref[...], own_low_ref[...] = own


def green_body(
    core_ref, other_ref, inter_ref, turned_high_ref, turned_low_ref, high_ref, low_ref, own_high_ref,
    own_low_ref, vector_ref, out_ref, kept_ref, inverse_ref, matrix_ref,
    solved_high_ref, solved_low_ref, sems, *, row_groups, col_groups
):
    core = core_ref[0]
    odd = core_ref[1]
    copies = []
    for sub in range(SUBS):
        rows = pl.ds(sub * SUB, SUB)
        for beside in range(2):
            cols = pl.ds((sub + beside) % SUBS * SUB, SUB)
            target = odd if beside == 0 else 1 - odd
            copies.append(
                pltpu.make_async_copy(
                    vector_ref.at[rows, cols, :],
                    kept_ref.at[rows, pl.ds(pl.multiple_of(target * SUB, SUB), SUB), :],
                    sems.at[2 * sub + beside],
                )
            )
            copies[-1].start()
    orbital_count, electron_count = high_ref.shape
    slab_rows = orbital_count // row_groups
    slab_cols = orbital_count // col_groups
    other = split_two(other_ref[...])
    inter_other = three_terms((turned_high_ref[...], turned_low_ref[...]), other)
    inter = jnp.concatenate([inter_ref[...], inter_other], axis=1)
    inverse_scale = 1.0 / jnp.max(jnp.abs(inter))
    inter = inter * inverse_scale
    matrix_ref[...] = inter
    turned = inter.T
    eye = eye_of(electron_count)
    normal = dot_three(turned, inter)
    both = dot_three(normal, jnp.concatenate([normal, turned], axis=1))
    square = both[:, :electron_count]
    step_scales = scales()
    largest = jnp.sqrt(jnp.sqrt(jnp.sum(square * square))) * 1.001
    alpha = (2.0 - LOW_START) / largest
    scale = step_scales[0]
    error = eye - (2.0 * scale * alpha) * normal + (scale * alpha * alpha) * square
    inverse = (scale * alpha) * (2.0 * turned - alpha * both[:, electron_count:])
    for scale in step_scales[1:-1]:
        both = dot_three(error, jnp.concatenate([error, inverse], axis=1))
        inverse = scale * (inverse + both[:, electron_count:])
        error = (1.0 - scale) * eye + scale * both[:, :electron_count]
    inverse_ref[...] = step_scales[-1] * (inverse + dot_three(error, inverse))

    def refine(carried):
        count, _ = carried
        current = inverse_ref[...]
        residual = eye_of(electron_count) - dot_three(current, matrix_ref[...])
        inverse_ref[...] = current + dot_three(residual, current)
        return count + 1, jnp.sum(residual * residual)

    lax.while_loop(
        lambda carried: jnp.logical_and(carried[0] < MOST_STEPS, carried[1] > RESIDUAL_BOUND**2),
        refine,
        (jnp.int32(0), jnp.float32(1e30)),
    )
    walker = [
        jnp.concatenate([own, there], axis=1)
        for own, there in zip((own_high_ref[...], own_low_ref[...]), other)
    ]
    inverse = inverse_ref[...] * inverse_scale
    solved_high_ref[...], solved_low_ref[...] = split_two(three_terms(walker, split_two(inverse)))
    part = SUB // 2
    trial_refs = (high_ref, low_ref)
    solved_refs = (solved_high_ref, solved_low_ref)
    for sub in range(SUBS):
        following = (sub + 1) % SUBS
        starts = [
            pl.multiple_of(row * slab_rows + sub * SUB + core * part, part) for row in range(row_groups)
        ]
        same = [col * slab_cols + sub * SUB for col in range(col_groups)]
        beside = [col * slab_cols + following * SUB for col in range(col_groups)]
        mixed = []
        for col in range(col_groups):
            mixed += [beside[col], same[col]] if col % 2 else [same[col], beside[col]]

        def rows_of(refs, places, size):
            return [jnp.concatenate([ref[pl.ds(at, size), :] for at in places], axis=0) for ref in refs]

        green = three_terms(
            rows_of(solved_refs, starts, part), rows_of(trial_refs, mixed, SUB), last_dims
        )
        turned = three_terms(
            rows_of(trial_refs, starts, part), rows_of(solved_refs, beside, SUB), last_dims
        )
        for col in range(col_groups):
            tile = green[:, col * LANES : (col + 1) * LANES].astype(bf16).astype(f32)
            lane = col // 2 * LANES
            added = half_rolled(turned[:, lane : lane + LANES]).astype(bf16).astype(f32)
            first = tail_lanes(tile)
            plain, summed = tile, tile + added
            summed = jnp.where(first, summed, plain) if col % 2 else jnp.where(first, plain, summed)
            summed = summed.astype(bf16)
            for row in range(row_groups):
                out_ref[row * col_groups + col, sub * part : (sub + 1) * part, :] = summed[
                    row * part : (row + 1) * part
                ]
    for copy in copies:
        copy.wait()


def kept_rows(kept_ref, sub, place):
    part = SUB // 2
    start = pl.multiple_of(sub * SUB + place * part, part)
    return kept_ref[pl.ds(start, part)].reshape(part * LANES, kept_ref.shape[2])


def bias_body(place_ref, green_ref, kept_ref, before_ref, out_ref, turned_ref):
    part = SUB // 2
    place = place_ref[0]
    turned_ref[...] = jnp.swapaxes(green_ref[...].astype(f32), 0, 1).astype(bf16)
    total = before_ref[...]
    for sub in range(SUBS):
        left = [turned_ref[sub * part + row] for row in range(part)]
        total = total + dot_of(jnp.concatenate(left, axis=1), kept_rows(kept_ref, sub, place))
    for device in range(out_ref.shape[0]):
        out_ref[device] = total


def potential_body(place_ref, parts_ref, noise_ref, kept_ref, bias_ref, out_ref):
    part = SUB // 2
    place = place_ref[0]
    walker_total = noise_ref.shape[0]
    bias = parts_ref[0]
    for device in range(1, parts_ref.shape[0]):
        bias = bias + parts_ref[device]
    bias_ref[...] = bias
    high, low = split_two(noise_ref[...] + root_step * bias)
    weights = jnp.concatenate([high, low], axis=0)
    for sub in range(SUBS):
        both = dot_of(weights, kept_rows(kept_ref, sub, place), last_dims)
        added = both[:walker_total] + both[walker_total:]
        for row in range(part):
            out_ref[sub * part + row] = added[:, row * LANES : (row + 1) * LANES]


def joined_tiles(source_ref, sub, row, col_groups):
    part = SUB // 2
    same = []
    beside = []
    for col in range(0, col_groups, 2):
        index = row * col_groups + col
        even = source_ref[index, sub * part : (sub + 1) * part, :]
        odd = source_ref[index + 1, sub * part : (sub + 1) * part, :]
        same.append(jnp.where(tail_lanes(even), even, odd))
        beside.append(half_rolled(jnp.where(tail_lanes(even), odd, even).astype(f32)).astype(bf16))
    return jnp.concatenate(same + beside, axis=1)


def joined_body(source_ref, out_ref, *, row_groups, col_groups):
    for sub in range(SUBS):
        for row in range(row_groups):
            out_ref[sub * row_groups + row] = joined_tiles(source_ref, sub, row, col_groups)


def series_body(core_ref, joined_ref, other_ref, walker_ref, out_ref, matrix_ref, stage_ref, sems, *, row_groups, col_groups):
    slab = SUB * SUBS
    part = SUB // 2
    size = row_groups * SUB
    core = core_ref[0]
    for place in range(2):
        for sub in range(SUBS):
            lane = (sub + 1) % SUBS * size
            for row in range(row_groups):
                if place == 0:
                    tiles = joined_ref[sub * row_groups + row]
                    shift = core * part
                else:
                    tiles = joined_tiles(other_ref, sub, row, col_groups)
                    shift = (1 - core) * part
                rows = pl.ds(pl.multiple_of(sub * size + row * SUB + shift, part), part)
                matrix_ref[rows, sub * size : (sub + 1) * size] = tiles[:, :size]
                matrix_ref[rows, lane : lane + size] = tiles[:, size:]
    for sub in range(SUBS):
        following = (sub + 1) % SUBS
        block = matrix_ref[sub * size : (sub + 1) * size, following * size : (following + 1) * size]
        matrix_ref[following * size : (following + 1) * size, sub * size : (sub + 1) * size] = block.T

    pieces = []
    for sub in range(SUBS):
        for row in range(row_groups):
            pieces.append(walker_ref[row * slab + sub * SUB : row * slab + (sub + 1) * SUB, :])
    term = jnp.concatenate(pieces, axis=0)
    total = term
    width = term.shape[1]
    for degree in range(1, TERMS - 1):
        right = jnp.concatenate(split_two(term), axis=1)
        both = dot_of(matrix_ref[...], right)
        term = (-root_step / degree) * (both[:, :width] + both[:, width:])
        total = total + term
    right = jnp.concatenate(split_two(term), axis=1)
    copies = []
    for sub in range(SUBS):
        rows = slice(sub * size, (sub + 1) * size)
        both = dot_of(matrix_ref[rows, :], right)
        term = (-root_step / (TERMS - 1)) * (both[:, :width] + both[:, width:])
        stage_ref[rows, :] = total[rows] + term
        for row in range(row_groups):
            copies.append(
                pltpu.make_async_copy(
                    stage_ref.at[pl.ds(sub * size + row * SUB, SUB), :],
                    out_ref.at[pl.ds(row * slab + sub * SUB, SUB), :],
                    sems.at[sub * row_groups + row],
                )
            )
            copies[-1].start()
    for copy in copies:
        copy.wait()


smem = pl.BlockSpec(memory_space=pltpu.SMEM)
vmem = pl.BlockSpec(memory_space=pltpu.VMEM)
anywhere = pl.BlockSpec(memory_space=pl.ANY)
grant = pltpu.CompilerParams(vmem_limit_bytes=20 * 2**20)


def bias_half(place, green, kept, before, copies):
    owners, dense, _ = green.shape
    held = kept.shape[2]
    return pl.pallas_call(
        bias_body,
        in_specs=[smem, vmem, vmem, vmem],
        out_specs=vmem,
        scratch_shapes=[pltpu.VMEM((dense, owners, LANES), bf16)],
        out_shape=jax.ShapeDtypeStruct((copies, owners, held), f32),
        compiler_params=grant,
        name="bias",
    )(place, green, in_vmem(kept), before)


def in_hbm(value):
    return pltpu.with_memory_space_constraint(value, pltpu.HBM)


def in_vmem(value):
    return pltpu.with_memory_space_constraint(value, pltpu.VMEM)


def potential_half(place, parts, noise, kept):
    _, owners, held = parts.shape
    return pl.pallas_call(
        potential_body,
        in_specs=[smem, vmem, vmem, vmem],
        out_specs=(vmem, vmem),
        out_shape=(
            jax.ShapeDtypeStruct((owners, held), f32),
            jax.ShapeDtypeStruct((SUBS * SUB // 2, owners, LANES), f32),
        ),
        compiler_params=grant,
        name="potential",
    )(place, parts, noise, in_vmem(kept))


def fast_shards(chol_vectors, trial_orbitals, walkers, field_noise):
    held = chol_vectors.shape[0]
    orbital_count, electron_count = trial_orbitals.shape
    row_groups = lax.axis_size("pairs")
    col_groups = lax.axis_size("chol")
    owners = row_groups * col_groups
    dense = SUBS * SUB // 2
    core = lax.axis_index("walk").astype(jnp.int32).reshape(1)
    parity = (lax.axis_index("chol").astype(jnp.int32) % 2).reshape(1)
    vectors = jnp.transpose(chol_vectors, (1, 2, 0))
    own = walkers[0]
    other = swapped(own, "walk", 0)
    early = pl.pallas_call(
        overlap_body,
        out_shape=[jax.ShapeDtypeStruct((electron_count, own.shape[1]), f32)]
        + [jax.ShapeDtypeStruct((electron_count, orbital_count), bf16)] * 2
        + [jax.ShapeDtypeStruct(trial_orbitals.shape, bf16)] * 2
        + [jax.ShapeDtypeStruct(own.shape, bf16)] * 2,
        in_specs=[vmem, vmem],
        out_specs=[vmem] * 7,
        compiler_params=grant,
        name="overlap",
    )(in_hbm(own), in_hbm(trial_orbitals))
    square = (electron_count, electron_count)
    outgoing, kept = pl.pallas_call(
        functools.partial(green_body, row_groups=row_groups, col_groups=col_groups),
        out_shape=(
            jax.ShapeDtypeStruct((owners, dense, LANES), bf16),
            pltpu.VMEM((SUBS * SUB, LANES, held), bf16),
        ),
        in_specs=[smem] + [vmem] * 8 + [anywhere],
        out_specs=(vmem, vmem),
        scratch_shapes=[
            pltpu.VMEM(square, f32),
            pltpu.VMEM(square, f32),
            pltpu.VMEM(trial_orbitals.shape, bf16),
            pltpu.VMEM(trial_orbitals.shape, bf16),
            pltpu.SemaphoreType.DMA((2 * SUBS,)),
        ],
        compiler_params=grant,
        name="green",
    )(jnp.concatenate([core, parity]), other, *early, in_hbm(vectors))
    axes = ("pairs", "chol")
    arrived = lax.all_to_all(outgoing, axes, split_axis=0, concat_axis=0, tiled=True)
    arrived_other = swapped(arrived, "walk", 0)
    first = bias_half(core, arrived, kept, jnp.zeros((owners, held), f32), 1)
    spread = bias_half(1 - core, arrived_other, kept, first[0], owners)
    parts = lax.all_to_all(spread, axes, split_axis=0, concat_axis=0, tiled=True)
    force_bias, send = potential_half(1 - core, parts, field_noise[0], kept)
    _, keep = potential_half(core, parts, field_noise[0], kept)
    summed = jnp.swapaxes((keep + swapped(send, "walk", 0)).astype(bf16), 0, 1)
    received = lax.all_to_all(summed, axes, split_axis=0, concat_axis=0, tiled=True)
    received_other = swapped(received, "walk", 0)
    sizes = dict(row_groups=row_groups, col_groups=col_groups)
    joined = pl.pallas_call(
        functools.partial(joined_body, **sizes),
        out_shape=jax.ShapeDtypeStruct((SUBS * row_groups, SUB // 2, 2 * SUB * col_groups), bf16),
        in_specs=[vmem],
        out_specs=vmem,
        compiler_params=grant,
        name="joined",
    )(received)
    propagated = pl.pallas_call(
        functools.partial(series_body, **sizes),
        out_shape=jax.ShapeDtypeStruct(own.shape, f32),
        in_specs=[smem, vmem, vmem, vmem],
        out_specs=anywhere,
        scratch_shapes=[
            pltpu.VMEM((orbital_count, orbital_count), bf16),
            pltpu.VMEM(own.shape, f32),
            pltpu.SemaphoreType.DMA((SUBS * row_groups,)),
        ],
        compiler_params=grant,
        name="series",
    )(core, joined, received_other, own)
    return propagated[None], force_bias[None]


def packable(chol_vectors, trial_orbitals, walkers, field_noise):
    held, slab_rows, slab_cols = chol_vectors.shape
    row_groups = lax.axis_size("pairs")
    return (
        walkers.shape[0] == 1
        and lax.axis_size("walk") == 2
        and lax.axis_size("chol") == row_groups
        and row_groups in (2, 4, 8)
        and slab_cols == slab_rows == SUB * SUBS
        and held % LANES == 0
        and trial_orbitals.shape[1] % LANES == 0
        and field_noise.shape[0] == 1
    )


def chosen_shards(*args):
    return fast_shards(*args) if packable(*args) else shards(*args)


def solution(mesh):
    placed = (
        P(("groups", "walk"), "pairs", "chol"),
        P("groups", None),
        P(("groups", "pairs", "chol"), None, "walk"),
        P("groups", None, "walk"),
    )
    return jax.shard_map(
        chosen_shards,
        mesh=mesh,
        in_specs=placed,
        out_specs=(P(("groups", "pairs", "chol"), None, "walk"), P("groups", None, "walk")),
        check_vma=False,
    )
```

```python
import functools

import jax
import jax.numpy as jnp
from jax import lax
from jax.experimental import pallas as pl
from jax.experimental.pallas import tpu as pltpu
from jax.sharding import PartitionSpec as P

TERMS = 6


root_step = 0.05
highest = lax.Precision.HIGHEST
LANES = 128
SUB = LANES // 2
SUBS = 3
f32 = jnp.float32
bf16 = jnp.bfloat16


def swapped(value, axis, apart):
    mask = 2**apart
    pairs = [(source, source ^ mask) for source in range(lax.axis_size(axis))]
    return lax.ppermute(value, axis, pairs)


def solve_normal(factor, right_side):
    middle = lax.linalg.triangular_solve(factor, right_side, left_side=True, lower=True)
    return lax.linalg.triangular_solve(factor, middle, left_side=True, lower=True, transpose_a=True)


def green_blocks(walker_full, trial_orbitals, trial_part, row_groups, col_groups):
    owner_walkers, orbital_count, electron_count = walker_full.shape
    intersection = jnp.einsum("nm,wnk->wmk", trial_orbitals, walker_full, precision=highest)
    normal = jnp.einsum("wmk,wml->wkl", intersection, intersection, precision=highest)
    factor = jnp.linalg.cholesky(normal)
    rotated = jnp.einsum("wmk,cbm->wkcb", intersection, trial_part, precision=highest)
    chosen_cols = rotated.shape[2] * rotated.shape[3]
    solved = solve_normal(factor, rotated.reshape(owner_walkers, electron_count, chosen_cols))
    slab_rows = orbital_count // row_groups
    block_cols = chosen_cols // col_groups
    shaped = solved.reshape(owner_walkers, electron_count, col_groups, block_cols)
    walker_rows = walker_full.reshape(owner_walkers, row_groups, slab_rows, electron_count)
    blocks = jnp.einsum("wiak,wkcb->icwab", walker_rows, shaped, precision=highest)
    return blocks.astype(jnp.bfloat16).reshape(
        row_groups * col_groups, owner_walkers, slab_rows * block_cols
    )


def shards(chol_vectors, trial_orbitals, walkers, field_noise):
    held_vectors, slab_rows, slab_cols = chol_vectors.shape
    owner_walkers = walkers.shape[0]
    orbital_count = walkers.shape[1]
    electron_count = trial_orbitals.shape[1]
    row_groups = lax.axis_size("pairs")
    col_groups = lax.axis_size("chol")
    core_count = lax.axis_size("walk")
    core_index = lax.axis_index("walk")
    core_cols = slab_cols // core_count
    owner_count = row_groups * col_groups
    walker_total = owner_count * owner_walkers
    flat_vectors = chol_vectors.reshape(held_vectors, slab_rows * slab_cols)
    trial_split = trial_orbitals.reshape(col_groups, core_count, core_cols, electron_count)
    trial_part = lax.dynamic_index_in_dim(trial_split, core_index, 1, keepdims=False)
    walker_full = lax.all_gather(walkers, "walk", axis=2, tiled=True)
    outgoing = green_blocks(walker_full, trial_orbitals, trial_part, row_groups, col_groups)
    sectioned = outgoing.reshape(row_groups, col_groups, owner_walkers, slab_rows * core_cols)
    arrived = lax.all_to_all(
        lax.all_to_all(sectioned, "pairs", split_axis=0, concat_axis=0, tiled=True),
        "chol",
        split_axis=1,
        concat_axis=1,
        tiled=True,
    )
    arrived = arrived.reshape(walker_total, slab_rows, core_cols)
    partial_bias = jnp.einsum(
        "wab,gab->wg",
        lax.all_gather(arrived, "walk", axis=2, tiled=True),
        chol_vectors,
        preferred_element_type=jnp.float32,
    )
    force_bias = lax.psum(partial_bias, ("pairs", "chol"))
    bias_steps = [force_bias]
    shifted = field_noise[0] + root_step * force_bias
    shifted_high = lax.optimization_barrier(shifted.astype(jnp.bfloat16))
    shifted_low = (shifted - shifted_high.astype(jnp.float32)).astype(jnp.bfloat16)
    stacked = jnp.stack([shifted_high, shifted_low])
    both_parts = lax.dot_general(
        stacked, flat_vectors, (((2,), (0,)), ((), ())), preferred_element_type=jnp.float32
    )
    potential = both_parts[0] + both_parts[1]
    blocks_out = potential.reshape(owner_count, owner_walkers, slab_rows * slab_cols)
    received = lax.all_to_all(
        blocks_out, ("pairs", "chol"), split_axis=0, concat_axis=0, tiled=True
    )
    partner = swapped(received, "walk", 0)
    summed = (received + partner).reshape(
        row_groups, col_groups, owner_walkers, slab_rows, core_count, core_cols
    )
    matrix = jnp.transpose(summed, (2, 0, 3, 1, 4, 5)).reshape(
        owner_walkers, orbital_count, orbital_count
    )
    running_term = walkers
    running_sum = walkers
    for degree in range(1, TERMS):
        running_term = -(root_step / degree) * jnp.einsum(
            "wpq,wqm->wpm", matrix, running_term, precision=highest
        )
        running_sum = running_sum + running_term
    return (running_sum, jnp.stack(bias_steps))


def split_two(value):
    high = value.astype(bf16)
    return high, (value - high.astype(f32)).astype(bf16)


def dot_of(left, right, dims=(((1,), (0,)), ((), ())), precision=None):
    return lax.dot_general(left, right, dims, precision=precision, preferred_element_type=f32)


def dot_three(left, right):
    left_high, left_low = split_two(left)
    right_high, right_low = split_two(right)
    return dot_of(
        jnp.concatenate([left_high, left_low, left_high], axis=1),
        jnp.concatenate([right_high, right_high, right_low], axis=0),
    )


first_dims = (((0,), (0,)), ((), ()))
last_dims = (((1,), (1,)), ((), ()))


def eye_of(size):
    rows = lax.broadcasted_iota(jnp.int32, (size, size), 0)
    cols = lax.broadcasted_iota(jnp.int32, (size, size), 1)
    return (rows == cols).astype(f32)


def half_rolled(value):
    return pltpu.roll(value, LANES // 2, 1)


def tail_lanes(value):
    return lax.broadcasted_iota(jnp.int32, value.shape, 1) < LANES // 2


LOW_START = 4e-4
PAIRED_STEPS = 7
RESIDUAL_BOUND = 2e-2
MOST_STEPS = 60


def scales():
    low = LOW_START
    found = []
    for _ in range(PAIRED_STEPS + 1):
        scale = 2.0 / (1.0 + 2.0 * low - low * low)
        found.append(scale)
        low = 2.0 - scale
    return found


def three_terms(left, right, dims=(((1,), (0,)), ((), ()))):
    count = left[0].shape[0]
    both = dot_of(jnp.concatenate(left, axis=0), right[0], dims)
    return both[:count] + both[count:] + dot_of(left[0], right[1], dims)


def overlap_body(own_ref, trial_ref, inter_ref, turned_high_ref, turned_low_ref, high_ref, low_ref, own_high_ref, own_low_ref):
    trial = trial_ref[...]
    own = split_two(own_ref[...])
    turned = split_two(trial.T)
    inter_ref[...] = three_terms(turned, own)
    turned_high_ref[...], turned_low_ref[...] = turned
    high_ref[...], low_ref[...] = split_two(trial)
    own_high_ref[...], own_low_ref[...] = own


def green_body(
    core_ref, other_ref, inter_ref, turned_high_ref, turned_low_ref, high_ref, low_ref, own_high_ref,
    own_low_ref, vector_ref, out_ref, kept_ref, inverse_ref, matrix_ref,
    solved_high_ref, solved_low_ref, sems, *, row_groups, col_groups
):
    core = core_ref[0]
    odd = core_ref[1]
    copies = []
    for sub in range(SUBS):
        rows = pl.ds(sub * SUB, SUB)
        for beside in range(2):
            cols = pl.ds((sub + beside) % SUBS * SUB, SUB)
            target = odd if beside == 0 else 1 - odd
            copies.append(
                pltpu.make_async_copy(
                    vector_ref.at[rows, cols, :],
                    kept_ref.at[rows, pl.ds(pl.multiple_of(target * SUB, SUB), SUB), :],
                    sems.at[2 * sub + beside],
                )
            )
            copies[-1].start()
    orbital_count, electron_count = high_ref.shape
    slab_rows = orbital_count // row_groups
    slab_cols = orbital_count // col_groups
    other = split_two(other_ref[...])
    inter_other = three_terms((turned_high_ref[...], turned_low_ref[...]), other)
    inter = jnp.concatenate([inter_ref[...], inter_other], axis=1)
    inverse_scale = 1.0 / jnp.max(jnp.abs(inter))
    inter = inter * inverse_scale
    matrix_ref[...] = inter
    turned = inter.T
    eye = eye_of(electron_count)
    normal = dot_three(turned, inter)
    both = dot_three(normal, jnp.concatenate([normal, turned], axis=1))
    square = both[:, :electron_count]
    step_scales = scales()
    largest = jnp.sqrt(jnp.sqrt(jnp.sum(square * square))) * 1.001
    alpha = (2.0 - LOW_START) / largest
    scale = step_scales[0]
    error = eye - (2.0 * scale * alpha) * normal + (scale * alpha * alpha) * square
    inverse = (scale * alpha) * (2.0 * turned - alpha * both[:, electron_count:])
    for scale in step_scales[1:-1]:
        both = dot_three(error, jnp.concatenate([error, inverse], axis=1))
        inverse = scale * (inverse + both[:, electron_count:])
        error = (1.0 - scale) * eye + scale * both[:, :electron_count]
    inverse_ref[...] = step_scales[-1] * (inverse + dot_three(error, inverse))

    def refine(carried):
        count, _ = carried
        current = inverse_ref[...]
        residual = eye_of(electron_count) - dot_three(current, matrix_ref[...])
        inverse_ref[...] = current + dot_three(residual, current)
        return count + 1, jnp.sum(residual * residual)

    lax.while_loop(
        lambda carried: jnp.logical_and(carried[0] < MOST_STEPS, carried[1] > RESIDUAL_BOUND**2),
        refine,
        (jnp.int32(0), jnp.float32(1e30)),
    )
    walker = [
        jnp.concatenate([own, there], axis=1)
        for own, there in zip((own_high_ref[...], own_low_ref[...]), other)
    ]
    inverse = inverse_ref[...] * inverse_scale
    solved_high_ref[...], solved_low_ref[...] = split_two(three_terms(walker, split_two(inverse)))
    part = SUB // 2
    trial_refs = (high_ref, low_ref)
    solved_refs = (solved_high_ref, solved_low_ref)
    for sub in range(SUBS):
        following = (sub + 1) % SUBS
        starts = [
            pl.multiple_of(row * slab_rows + sub * SUB + core * part, part) for row in range(row_groups)
        ]
        same = [col * slab_cols + sub * SUB for col in range(col_groups)]
        beside = [col * slab_cols + following * SUB for col in range(col_groups)]
        mixed = []
        for col in range(col_groups):
            mixed += [beside[col], same[col]] if col % 2 else [same[col], beside[col]]

        def rows_of(refs, places, size):
            return [jnp.concatenate([ref[pl.ds(at, size), :] for at in places], axis=0) for ref in refs]

        green = three_terms(
            rows_of(solved_refs, starts, part), rows_of(trial_refs, mixed, SUB), last_dims
        )
        turned = three_terms(
            rows_of(trial_refs, starts, part), rows_of(solved_refs, beside, SUB), last_dims
        )
        for col in range(col_groups):
            tile = green[:, col * LANES : (col + 1) * LANES].astype(bf16).astype(f32)
            lane = col // 2 * LANES
            added = half_rolled(turned[:, lane : lane + LANES]).astype(bf16).astype(f32)
            first = tail_lanes(tile)
            plain, summed = tile, tile + added
            summed = jnp.where(first, summed, plain) if col % 2 else jnp.where(first, plain, summed)
            summed = summed.astype(bf16)
            for row in range(row_groups):
                out_ref[row * col_groups + col, sub * part : (sub + 1) * part, :] = summed[
                    row * part : (row + 1) * part
                ]
    for copy in copies:
        copy.wait()


def kept_rows(kept_ref, sub, place):
    part = SUB // 2
    start = pl.multiple_of(sub * SUB + place * part, part)
    return kept_ref[pl.ds(start, part)].reshape(part * LANES, kept_ref.shape[2])


def bias_body(place_ref, green_ref, kept_ref, before_ref, out_ref, turned_ref):
    part = SUB // 2
    place = place_ref[0]
    turned_ref[...] = jnp.swapaxes(green_ref[...].astype(f32), 0, 1).astype(bf16)
    total = before_ref[...]
    for sub in range(SUBS):
        left = [turned_ref[sub * part + row] for row in range(part)]
        total = total + dot_of(jnp.concatenate(left, axis=1), kept_rows(kept_ref, sub, place))
    for device in range(out_ref.shape[0]):
        out_ref[device] = total


def potential_body(place_ref, parts_ref, noise_ref, kept_ref, bias_ref, out_ref):
    part = SUB // 2
    place = place_ref[0]
    walker_total = noise_ref.shape[0]
    bias = parts_ref[0]
    for device in range(1, parts_ref.shape[0]):
        bias = bias + parts_ref[device]
    bias_ref[...] = bias
    high, low = split_two(noise_ref[...] + root_step * bias)
    weights = jnp.concatenate([high, low], axis=0)
    for sub in range(SUBS):
        both = dot_of(weights, kept_rows(kept_ref, sub, place), last_dims)
        added = both[:walker_total] + both[walker_total:]
        for row in range(part):
            out_ref[sub * part + row] = added[:, row * LANES : (row + 1) * LANES]


def joined_tiles(source_ref, sub, row, col_groups):
    part = SUB // 2
    same = []
    beside = []
    for col in range(0, col_groups, 2):
        index = row * col_groups + col
        even = source_ref[index, sub * part : (sub + 1) * part, :]
        odd = source_ref[index + 1, sub * part : (sub + 1) * part, :]
        same.append(jnp.where(tail_lanes(even), even, odd))
        beside.append(half_rolled(jnp.where(tail_lanes(even), odd, even).astype(f32)).astype(bf16))
    return jnp.concatenate(same + beside, axis=1)


def joined_body(source_ref, out_ref, *, row_groups, col_groups):
    for sub in range(SUBS):
        for row in range(row_groups):
            out_ref[sub * row_groups + row] = joined_tiles(source_ref, sub, row, col_groups)


def series_body(core_ref, joined_ref, other_ref, walker_ref, out_ref, matrix_ref, stage_ref, sems, *, row_groups, col_groups):
    slab = SUB * SUBS
    part = SUB // 2
    size = row_groups * SUB
    core = core_ref[0]
    for place in range(2):
        for sub in range(SUBS):
            lane = (sub + 1) % SUBS * size
            for row in range(row_groups):
                if place == 0:
                    tiles = joined_ref[sub * row_groups + row]
                    shift = core * part
                else:
                    tiles = joined_tiles(other_ref, sub, row, col_groups)
                    shift = (1 - core) * part
                rows = pl.ds(pl.multiple_of(sub * size + row * SUB + shift, part), part)
                matrix_ref[rows, sub * size : (sub + 1) * size] = tiles[:, :size]
                matrix_ref[rows, lane : lane + size] = tiles[:, size:]
    for sub in range(SUBS):
        following = (sub + 1) % SUBS
        block = matrix_ref[sub * size : (sub + 1) * size, following * size : (following + 1) * size]
        matrix_ref[following * size : (following + 1) * size, sub * size : (sub + 1) * size] = block.T

    pieces = []
    for sub in range(SUBS):
        for row in range(row_groups):
            pieces.append(walker_ref[row * slab + sub * SUB : row * slab + (sub + 1) * SUB, :])
    term = jnp.concatenate(pieces, axis=0).T
    total = term
    count = term.shape[0]
    for degree in range(1, TERMS):
        pair = split_two(term)
        if degree < 3:
            both = dot_of(jnp.concatenate(pair, axis=0), matrix_ref[...])
            both = both[:count] + both[count:]
        else:
            both = dot_of(pair[0], matrix_ref[...])
        term = (-root_step / degree) * both
        total = total + term
    copies = []
    for sub in range(SUBS):
        rows = slice(sub * size, (sub + 1) * size)
        stage_ref[rows, :] = total[:, rows].T
        for row in range(row_groups):
            copies.append(
                pltpu.make_async_copy(
                    stage_ref.at[pl.ds(sub * size + row * SUB, SUB), :],
                    out_ref.at[pl.ds(row * slab + sub * SUB, SUB), :],
                    sems.at[sub * row_groups + row],
                )
            )
            copies[-1].start()
    for copy in copies:
        copy.wait()


smem = pl.BlockSpec(memory_space=pltpu.SMEM)
vmem = pl.BlockSpec(memory_space=pltpu.VMEM)
anywhere = pl.BlockSpec(memory_space=pl.ANY)
grant = pltpu.CompilerParams(vmem_limit_bytes=20 * 2**20)


def bias_half(place, green, kept, before, copies):
    owners, dense, _ = green.shape
    held = kept.shape[2]
    return pl.pallas_call(
        bias_body,
        in_specs=[smem, vmem, vmem, vmem],
        out_specs=vmem,
        scratch_shapes=[pltpu.VMEM((dense, owners, LANES), bf16)],
        out_shape=jax.ShapeDtypeStruct((copies, owners, held), f32),
        compiler_params=grant,
        name="bias",
    )(place, green, in_vmem(kept), before)


def in_hbm(value):
    return pltpu.with_memory_space_constraint(value, pltpu.HBM)


def in_vmem(value):
    return pltpu.with_memory_space_constraint(value, pltpu.VMEM)


def potential_half(place, parts, noise, kept):
    _, owners, held = parts.shape
    return pl.pallas_call(
        potential_body,
        in_specs=[smem, vmem, vmem, vmem],
        out_specs=(vmem, vmem),
        out_shape=(
            jax.ShapeDtypeStruct((owners, held), f32),
            jax.ShapeDtypeStruct((SUBS * SUB // 2, owners, LANES), f32),
        ),
        compiler_params=grant,
        name="potential",
    )(place, parts, noise, in_vmem(kept))


def fast_shards(chol_vectors, trial_orbitals, walkers, field_noise):
    held = chol_vectors.shape[0]
    orbital_count, electron_count = trial_orbitals.shape
    row_groups = lax.axis_size("pairs")
    col_groups = lax.axis_size("chol")
    owners = row_groups * col_groups
    dense = SUBS * SUB // 2
    core = lax.axis_index("walk").astype(jnp.int32).reshape(1)
    parity = (lax.axis_index("chol").astype(jnp.int32) % 2).reshape(1)
    vectors = jnp.transpose(chol_vectors, (1, 2, 0))
    own = walkers[0]
    other = swapped(own, "walk", 0)
    early = pl.pallas_call(
        overlap_body,
        out_shape=[jax.ShapeDtypeStruct((electron_count, own.shape[1]), f32)]
        + [jax.ShapeDtypeStruct((electron_count, orbital_count), bf16)] * 2
        + [jax.ShapeDtypeStruct(trial_orbitals.shape, bf16)] * 2
        + [jax.ShapeDtypeStruct(own.shape, bf16)] * 2,
        in_specs=[vmem, vmem],
        out_specs=[vmem] * 7,
        compiler_params=grant,
        name="overlap",
    )(in_hbm(own), in_hbm(trial_orbitals))
    square = (electron_count, electron_count)
    outgoing, kept = pl.pallas_call(
        functools.partial(green_body, row_groups=row_groups, col_groups=col_groups),
        out_shape=(
            jax.ShapeDtypeStruct((owners, dense, LANES), bf16),
            pltpu.VMEM((SUBS * SUB, LANES, held), bf16),
        ),
        in_specs=[smem] + [vmem] * 8 + [anywhere],
        out_specs=(vmem, vmem),
        scratch_shapes=[
            pltpu.VMEM(square, f32),
            pltpu.VMEM(square, f32),
            pltpu.VMEM(trial_orbitals.shape, bf16),
            pltpu.VMEM(trial_orbitals.shape, bf16),
            pltpu.SemaphoreType.DMA((2 * SUBS,)),
        ],
        compiler_params=grant,
        name="green",
    )(jnp.concatenate([core, parity]), other, *early, in_hbm(vectors))
    axes = ("pairs", "chol")
    arrived = lax.all_to_all(outgoing, axes, split_axis=0, concat_axis=0, tiled=True)
    arrived_other = swapped(arrived, "walk", 0)
    first = bias_half(core, arrived, kept, jnp.zeros((owners, held), f32), 1)
    spread = bias_half(1 - core, arrived_other, kept, first[0], owners)
    parts = lax.all_to_all(spread, axes, split_axis=0, concat_axis=0, tiled=True)
    force_bias, send = potential_half(1 - core, parts, field_noise[0], kept)
    _, keep = potential_half(core, parts, field_noise[0], kept)
    summed = jnp.swapaxes((keep + swapped(send, "walk", 0)).astype(bf16), 0, 1)
    received = lax.all_to_all(summed, axes, split_axis=0, concat_axis=0, tiled=True)
    received_other = swapped(received, "walk", 0)
    sizes = dict(row_groups=row_groups, col_groups=col_groups)
    joined = pl.pallas_call(
        functools.partial(joined_body, **sizes),
        out_shape=jax.ShapeDtypeStruct((SUBS * row_groups, SUB // 2, 2 * SUB * col_groups), bf16),
        in_specs=[vmem],
        out_specs=vmem,
        compiler_params=grant,
        name="joined",
    )(received)
    propagated = pl.pallas_call(
        functools.partial(series_body, **sizes),
        out_shape=jax.ShapeDtypeStruct(own.shape, f32),
        in_specs=[smem, vmem, vmem, vmem],
        out_specs=anywhere,
        scratch_shapes=[
            pltpu.VMEM((orbital_count, orbital_count), bf16),
            pltpu.VMEM(own.shape, f32),
            pltpu.SemaphoreType.DMA((SUBS * row_groups,)),
        ],
        compiler_params=grant,
        name="series",
    )(core, joined, received_other, own)
    return propagated[None], force_bias[None]


def packable(chol_vectors, trial_orbitals, walkers, field_noise):
    held, slab_rows, slab_cols = chol_vectors.shape
    row_groups = lax.axis_size("pairs")
    return (
        walkers.shape[0] == 1
        and lax.axis_size("walk") == 2
        and lax.axis_size("chol") == row_groups
        and row_groups in (2, 4, 8)
        and slab_cols == slab_rows == SUB * SUBS
        and held % LANES == 0
        and trial_orbitals.shape[1] % LANES == 0
        and field_noise.shape[0] == 1
    )


def chosen_shards(*args):
    return fast_shards(*args) if packable(*args) else shards(*args)


def solution(mesh):
    placed = (
        P(("groups", "walk"), "pairs", "chol"),
        P("groups", None),
        P(("groups", "pairs", "chol"), None, "walk"),
        P("groups", None, "walk"),
    )
    return jax.shard_map(
        chosen_shards,
        mesh=mesh,
        in_specs=placed,
        out_specs=(P(("groups", "pairs", "chol"), None, "walk"), P("groups", None, "walk")),
        check_vma=False,
    )
```

```python
import functools

import jax
import jax.numpy as jnp
from jax import lax
from jax.experimental import pallas as pl
from jax.experimental.pallas import tpu as pltpu
from jax.sharding import PartitionSpec as P

TERMS = 6


root_step = 0.05
highest = lax.Precision.HIGHEST
LANES = 128
SUB = LANES // 2
SUBS = 3
f32 = jnp.float32
bf16 = jnp.bfloat16


def swapped(value, axis, apart):
    mask = 2**apart
    pairs = [(source, source ^ mask) for source in range(lax.axis_size(axis))]
    return lax.ppermute(value, axis, pairs)


def solve_normal(factor, right_side):
    middle = lax.linalg.triangular_solve(factor, right_side, left_side=True, lower=True)
    return lax.linalg.triangular_solve(factor, middle, left_side=True, lower=True, transpose_a=True)


def green_blocks(walker_full, trial_orbitals, trial_part, row_groups, col_groups):
    owner_walkers, orbital_count, electron_count = walker_full.shape
    intersection = jnp.einsum("nm,wnk->wmk", trial_orbitals, walker_full, precision=highest)
    normal = jnp.einsum("wmk,wml->wkl", intersection, intersection, precision=highest)
    factor = jnp.linalg.cholesky(normal)
    rotated = jnp.einsum("wmk,cbm->wkcb", intersection, trial_part, precision=highest)
    chosen_cols = rotated.shape[2] * rotated.shape[3]
    solved = solve_normal(factor, rotated.reshape(owner_walkers, electron_count, chosen_cols))
    slab_rows = orbital_count // row_groups
    block_cols = chosen_cols // col_groups
    shaped = solved.reshape(owner_walkers, electron_count, col_groups, block_cols)
    walker_rows = walker_full.reshape(owner_walkers, row_groups, slab_rows, electron_count)
    blocks = jnp.einsum("wiak,wkcb->icwab", walker_rows, shaped, precision=highest)
    return blocks.astype(jnp.bfloat16).reshape(
        row_groups * col_groups, owner_walkers, slab_rows * block_cols
    )


def shards(chol_vectors, trial_orbitals, walkers, field_noise):
    held_vectors, slab_rows, slab_cols = chol_vectors.shape
    owner_walkers = walkers.shape[0]
    orbital_count = walkers.shape[1]
    electron_count = trial_orbitals.shape[1]
    row_groups = lax.axis_size("pairs")
    col_groups = lax.axis_size("chol")
    core_count = lax.axis_size("walk")
    core_index = lax.axis_index("walk")
    core_cols = slab_cols // core_count
    owner_count = row_groups * col_groups
    walker_total = owner_count * owner_walkers
    flat_vectors = chol_vectors.reshape(held_vectors, slab_rows * slab_cols)
    trial_split = trial_orbitals.reshape(col_groups, core_count, core_cols, electron_count)
    trial_part = lax.dynamic_index_in_dim(trial_split, core_index, 1, keepdims=False)
    walker_full = lax.all_gather(walkers, "walk", axis=2, tiled=True)
    outgoing = green_blocks(walker_full, trial_orbitals, trial_part, row_groups, col_groups)
    sectioned = outgoing.reshape(row_groups, col_groups, owner_walkers, slab_rows * core_cols)
    arrived = lax.all_to_all(
        lax.all_to_all(sectioned, "pairs", split_axis=0, concat_axis=0, tiled=True),
        "chol",
        split_axis=1,
        concat_axis=1,
        tiled=True,
    )
    arrived = arrived.reshape(walker_total, slab_rows, core_cols)
    partial_bias = jnp.einsum(
        "wab,gab->wg",
        lax.all_gather(arrived, "walk", axis=2, tiled=True),
        chol_vectors,
        preferred_element_type=jnp.float32,
    )
    force_bias = lax.psum(partial_bias, ("pairs", "chol"))
    bias_steps = [force_bias]
    shifted = field_noise[0] + root_step * force_bias
    shifted_high = lax.optimization_barrier(shifted.astype(jnp.bfloat16))
    shifted_low = (shifted - shifted_high.astype(jnp.float32)).astype(jnp.bfloat16)
    stacked = jnp.stack([shifted_high, shifted_low])
    both_parts = lax.dot_general(
        stacked, flat_vectors, (((2,), (0,)), ((), ())), preferred_element_type=jnp.float32
    )
    potential = both_parts[0] + both_parts[1]
    blocks_out = potential.reshape(owner_count, owner_walkers, slab_rows * slab_cols)
    received = lax.all_to_all(
        blocks_out, ("pairs", "chol"), split_axis=0, concat_axis=0, tiled=True
    )
    partner = swapped(received, "walk", 0)
    summed = (received + partner).reshape(
        row_groups, col_groups, owner_walkers, slab_rows, core_count, core_cols
    )
    matrix = jnp.transpose(summed, (2, 0, 3, 1, 4, 5)).reshape(
        owner_walkers, orbital_count, orbital_count
    )
    running_term = walkers
    running_sum = walkers
    for degree in range(1, TERMS):
        running_term = -(root_step / degree) * jnp.einsum(
            "wpq,wqm->wpm", matrix, running_term, precision=highest
        )
        running_sum = running_sum + running_term
    return (running_sum, jnp.stack(bias_steps))


def split_two(value):
    high = value.astype(bf16)
    return high, (value - high.astype(f32)).astype(bf16)


def dot_of(left, right, dims=(((1,), (0,)), ((), ())), precision=None):
    return lax.dot_general(left, right, dims, precision=precision, preferred_element_type=f32)


def dot_three(left, right):
    left_high, left_low = split_two(left)
    right_high, right_low = split_two(right)
    return dot_of(
        jnp.concatenate([left_high, left_low, left_high], axis=1),
        jnp.concatenate([right_high, right_high, right_low], axis=0),
    )


first_dims = (((0,), (0,)), ((), ()))
last_dims = (((1,), (1,)), ((), ()))


def eye_of(size):
    rows = lax.broadcasted_iota(jnp.int32, (size, size), 0)
    cols = lax.broadcasted_iota(jnp.int32, (size, size), 1)
    return (rows == cols).astype(f32)


def half_rolled(value):
    return pltpu.roll(value, LANES // 2, 1)


def tail_lanes(value):
    return lax.broadcasted_iota(jnp.int32, value.shape, 1) < LANES // 2


LOW_START = 4e-4
PAIRED_STEPS = 7
RESIDUAL_BOUND = 2e-2
MOST_STEPS = 60


def scales():
    low = LOW_START
    found = []
    for _ in range(PAIRED_STEPS + 1):
        scale = 2.0 / (1.0 + 2.0 * low - low * low)
        found.append(scale)
        low = 2.0 - scale
    return found


def three_terms(left, right, dims=(((1,), (0,)), ((), ()))):
    count = left[0].shape[0]
    both = dot_of(jnp.concatenate(left, axis=0), right[0], dims)
    return both[:count] + both[count:] + dot_of(left[0], right[1], dims)


def overlap_body(own_ref, trial_ref, inter_ref, turned_high_ref, turned_low_ref, high_ref, low_ref, own_high_ref, own_low_ref):
    trial = trial_ref[...]
    own = split_two(own_ref[...])
    turned = split_two(trial.T)
    inter_ref[...] = three_terms(turned, own)
    turned_high_ref[...], turned_low_ref[...] = turned
    high_ref[...], low_ref[...] = split_two(trial)
    own_high_ref[...], own_low_ref[...] = own


def green_body(
    core_ref, other_ref, inter_ref, turned_high_ref, turned_low_ref, high_ref, low_ref, own_high_ref,
    own_low_ref, vector_ref, out_ref, kept_ref, inverse_ref, matrix_ref,
    solved_high_ref, solved_low_ref, sems, *, row_groups, col_groups
):
    core = core_ref[0]
    odd = core_ref[1]
    copies = []
    for sub in range(SUBS):
        rows = pl.ds(sub * SUB, SUB)
        for beside in range(2):
            cols = pl.ds((sub + beside) % SUBS * SUB, SUB)
            target = odd if beside == 0 else 1 - odd
            copies.append(
                pltpu.make_async_copy(
                    vector_ref.at[rows, cols, :],
                    kept_ref.at[rows, pl.ds(pl.multiple_of(target * SUB, SUB), SUB), :],
                    sems.at[2 * sub + beside],
                )
            )
            copies[-1].start()
    orbital_count, electron_count = high_ref.shape
    slab_rows = orbital_count // row_groups
    slab_cols = orbital_count // col_groups
    other = split_two(other_ref[...])
    inter_other = three_terms((turned_high_ref[...], turned_low_ref[...]), other)
    inter = jnp.concatenate([inter_ref[...], inter_other], axis=1)
    inverse_scale = 1.0 / jnp.max(jnp.abs(inter))
    inter = inter * inverse_scale
    matrix_ref[...] = inter
    turned = inter.T
    eye = eye_of(electron_count)
    normal = dot_three(turned, inter)
    both = dot_three(normal, jnp.concatenate([normal, turned], axis=1))
    square = both[:, :electron_count]
    step_scales = scales()
    largest = jnp.sqrt(jnp.sqrt(jnp.sum(square * square))) * 1.001
    alpha = (2.0 - LOW_START) / largest
    scale = step_scales[0]
    error = eye - (2.0 * scale * alpha) * normal + (scale * alpha * alpha) * square
    inverse = (scale * alpha) * (2.0 * turned - alpha * both[:, electron_count:])
    for scale in step_scales[1:-1]:
        both = dot_three(error, jnp.concatenate([error, inverse], axis=1))
        inverse = scale * (inverse + both[:, electron_count:])
        error = (1.0 - scale) * eye + scale * both[:, :electron_count]
    inverse_ref[...] = step_scales[-1] * (inverse + dot_three(error, inverse))

    def refine(carried):
        count, _ = carried
        current = inverse_ref[...]
        residual = eye_of(electron_count) - dot_three(current, matrix_ref[...])
        inverse_ref[...] = current + dot_three(residual, current)
        return count + 1, jnp.sum(residual * residual)

    lax.while_loop(
        lambda carried: jnp.logical_and(carried[0] < MOST_STEPS, carried[1] > RESIDUAL_BOUND**2),
        refine,
        (jnp.int32(0), jnp.float32(1e30)),
    )
    walker = [
        jnp.concatenate([own, there], axis=1)
        for own, there in zip((own_high_ref[...], own_low_ref[...]), other)
    ]
    inverse = inverse_ref[...] * inverse_scale
    solved_high_ref[...], solved_low_ref[...] = split_two(three_terms(walker, split_two(inverse)))
    part = SUB // 2
    trial_refs = (high_ref, low_ref)
    solved_refs = (solved_high_ref, solved_low_ref)
    for sub in range(SUBS):
        following = (sub + 1) % SUBS
        starts = [
            pl.multiple_of(row * slab_rows + sub * SUB + core * part, part) for row in range(row_groups)
        ]
        same = [col * slab_cols + sub * SUB for col in range(col_groups)]
        beside = [col * slab_cols + following * SUB for col in range(col_groups)]
        mixed = []
        for col in range(col_groups):
            mixed += [beside[col], same[col]] if col % 2 else [same[col], beside[col]]

        def rows_of(refs, places, size):
            return [jnp.concatenate([ref[pl.ds(at, size), :] for at in places], axis=0) for ref in refs]

        green = three_terms(
            rows_of(solved_refs, starts, part), rows_of(trial_refs, mixed, SUB), last_dims
        )
        turned = three_terms(
            rows_of(trial_refs, starts, part), rows_of(solved_refs, beside, SUB), last_dims
        )
        for col in range(col_groups):
            tile = green[:, col * LANES : (col + 1) * LANES].astype(bf16).astype(f32)
            lane = col // 2 * LANES
            added = half_rolled(turned[:, lane : lane + LANES]).astype(bf16).astype(f32)
            first = tail_lanes(tile)
            plain, summed = tile, tile + added
            summed = jnp.where(first, summed, plain) if col % 2 else jnp.where(first, plain, summed)
            summed = summed.astype(bf16)
            for row in range(row_groups):
                out_ref[row * col_groups + col, sub * part : (sub + 1) * part, :] = summed[
                    row * part : (row + 1) * part
                ]
    for copy in copies:
        copy.wait()


def kept_rows(kept_ref, sub, place):
    part = SUB // 2
    start = pl.multiple_of(sub * SUB + place * part, part)
    return kept_ref[pl.ds(start, part)].reshape(part * LANES, kept_ref.shape[2])


def bias_body(place_ref, green_ref, kept_ref, before_ref, out_ref, turned_ref):
    part = SUB // 2
    place = place_ref[0]
    turned_ref[...] = jnp.swapaxes(green_ref[...].astype(f32), 0, 1).astype(bf16)
    total = before_ref[...]
    for sub in range(SUBS):
        left = [turned_ref[sub * part + row] for row in range(part)]
        total = total + dot_of(jnp.concatenate(left, axis=1), kept_rows(kept_ref, sub, place))
    for device in range(out_ref.shape[0]):
        out_ref[device] = total


def potential_body(place_ref, parts_ref, noise_ref, kept_ref, bias_ref, out_ref):
    part = SUB // 2
    place = place_ref[0]
    walker_total = noise_ref.shape[0]
    bias = parts_ref[0]
    for device in range(1, parts_ref.shape[0]):
        bias = bias + parts_ref[device]
    bias_ref[...] = bias
    high, low = split_two(noise_ref[...] + root_step * bias)
    weights = jnp.concatenate([high, low], axis=0)
    for sub in range(SUBS):
        both = dot_of(weights, kept_rows(kept_ref, sub, place), last_dims)
        added = both[:walker_total] + both[walker_total:]
        for row in range(part):
            out_ref[sub * part + row] = added[:, row * LANES : (row + 1) * LANES]


def joined_tiles(source_ref, sub, row, col_groups):
    part = SUB // 2
    same = []
    beside = []
    for col in range(0, col_groups, 2):
        index = row * col_groups + col
        even = source_ref[index, sub * part : (sub + 1) * part, :]
        odd = source_ref[index + 1, sub * part : (sub + 1) * part, :]
        same.append(jnp.where(tail_lanes(even), even, odd))
        beside.append(half_rolled(jnp.where(tail_lanes(even), odd, even).astype(f32)).astype(bf16))
    return jnp.concatenate(same + beside, axis=1)


def joined_body(source_ref, walker_ref, out_ref, turned_ref, pair_ref, *, row_groups, col_groups):
    for sub in range(SUBS):
        for row in range(row_groups):
            out_ref[sub * row_groups + row] = joined_tiles(source_ref, sub, row, col_groups)
    slab = SUB * SUBS
    pieces = []
    for sub in range(SUBS):
        for row in range(row_groups):
            pieces.append(walker_ref[row * slab + sub * SUB : row * slab + (sub + 1) * SUB, :])
    term = jnp.concatenate(pieces, axis=0).T
    turned_ref[...] = term
    pair_ref[...] = jnp.concatenate(split_two(term), axis=0)


def series_body(core_ref, joined_ref, turned_ref, pair_ref, other_ref, out_ref, matrix_ref, stage_ref, sems, *, row_groups, col_groups):
    slab = SUB * SUBS
    part = SUB // 2
    size = row_groups * SUB
    core = core_ref[0]
    for place in range(2):
        for sub in range(SUBS):
            lane = (sub + 1) % SUBS * size
            for row in range(row_groups):
                if place == 0:
                    tiles = joined_ref[sub * row_groups + row]
                    shift = core * part
                else:
                    tiles = joined_tiles(other_ref, sub, row, col_groups)
                    shift = (1 - core) * part
                rows = pl.ds(pl.multiple_of(sub * size + row * SUB + shift, part), part)
                matrix_ref[rows, sub * size : (sub + 1) * size] = tiles[:, :size]
                matrix_ref[rows, lane : lane + size] = tiles[:, size:]
    for sub in range(SUBS):
        following = (sub + 1) % SUBS
        block = matrix_ref[sub * size : (sub + 1) * size, following * size : (following + 1) * size]
        matrix_ref[following * size : (following + 1) * size, sub * size : (sub + 1) * size] = block.T

    total = turned_ref[...]
    count = total.shape[0]
    left = pair_ref[...]
    for degree in range(1, TERMS):
        both = dot_of(left, matrix_ref[...])
        if degree < 3:
            both = both[:count] + both[count:]
        term = (-root_step / degree) * both
        total = total + term
        left = jnp.concatenate(split_two(term), axis=0) if degree == 1 else term.astype(bf16)
    copies = []
    for sub in range(SUBS):
        rows = slice(sub * size, (sub + 1) * size)
        stage_ref[rows, :] = total[:, rows].T
        for row in range(row_groups):
            copies.append(
                pltpu.make_async_copy(
                    stage_ref.at[pl.ds(sub * size + row * SUB, SUB), :],
                    out_ref.at[pl.ds(row * slab + sub * SUB, SUB), :],
                    sems.at[sub * row_groups + row],
                )
            )
            copies[-1].start()
    for copy in copies:
        copy.wait()


smem = pl.BlockSpec(memory_space=pltpu.SMEM)
vmem = pl.BlockSpec(memory_space=pltpu.VMEM)
anywhere = pl.BlockSpec(memory_space=pl.ANY)
grant = pltpu.CompilerParams(vmem_limit_bytes=20 * 2**20)


def bias_half(place, green, kept, before, copies):
    owners, dense, _ = green.shape
    held = kept.shape[2]
    return pl.pallas_call(
        bias_body,
        in_specs=[smem, vmem, vmem, vmem],
        out_specs=vmem,
        scratch_shapes=[pltpu.VMEM((dense, owners, LANES), bf16)],
        out_shape=jax.ShapeDtypeStruct((copies, owners, held), f32),
        compiler_params=grant,
        name="bias",
    )(place, green, in_vmem(kept), before)


def in_hbm(value):
    return pltpu.with_memory_space_constraint(value, pltpu.HBM)


def in_vmem(value):
    return pltpu.with_memory_space_constraint(value, pltpu.VMEM)


def potential_half(place, parts, noise, kept):
    _, owners, held = parts.shape
    return pl.pallas_call(
        potential_body,
        in_specs=[smem, vmem, vmem, vmem],
        out_specs=(vmem, vmem),
        out_shape=(
            jax.ShapeDtypeStruct((owners, held), f32),
            jax.ShapeDtypeStruct((SUBS * SUB // 2, owners, LANES), f32),
        ),
        compiler_params=grant,
        name="potential",
    )(place, parts, noise, in_vmem(kept))


def fast_shards(chol_vectors, trial_orbitals, walkers, field_noise):
    held = chol_vectors.shape[0]
    orbital_count, electron_count = trial_orbitals.shape
    row_groups = lax.axis_size("pairs")
    col_groups = lax.axis_size("chol")
    owners = row_groups * col_groups
    dense = SUBS * SUB // 2
    core = lax.axis_index("walk").astype(jnp.int32).reshape(1)
    parity = (lax.axis_index("chol").astype(jnp.int32) % 2).reshape(1)
    vectors = jnp.transpose(chol_vectors, (1, 2, 0))
    own = walkers[0]
    other = swapped(own, "walk", 0)
    early = pl.pallas_call(
        overlap_body,
        out_shape=[jax.ShapeDtypeStruct((electron_count, own.shape[1]), f32)]
        + [jax.ShapeDtypeStruct((electron_count, orbital_count), bf16)] * 2
        + [jax.ShapeDtypeStruct(trial_orbitals.shape, bf16)] * 2
        + [jax.ShapeDtypeStruct(own.shape, bf16)] * 2,
        in_specs=[vmem, vmem],
        out_specs=[vmem] * 7,
        compiler_params=grant,
        name="overlap",
    )(in_hbm(own), in_hbm(trial_orbitals))
    square = (electron_count, electron_count)
    outgoing, kept = pl.pallas_call(
        functools.partial(green_body, row_groups=row_groups, col_groups=col_groups),
        out_shape=(
            jax.ShapeDtypeStruct((owners, dense, LANES), bf16),
            pltpu.VMEM((SUBS * SUB, LANES, held), bf16),
        ),
        in_specs=[smem] + [vmem] * 8 + [anywhere],
        out_specs=(vmem, vmem),
        scratch_shapes=[
            pltpu.VMEM(square, f32),
            pltpu.VMEM(square, f32),
            pltpu.VMEM(trial_orbitals.shape, bf16),
            pltpu.VMEM(trial_orbitals.shape, bf16),
            pltpu.SemaphoreType.DMA((2 * SUBS,)),
        ],
        compiler_params=grant,
        name="green",
    )(jnp.concatenate([core, parity]), other, *early, in_hbm(vectors))
    axes = ("pairs", "chol")
    arrived = lax.all_to_all(outgoing, axes, split_axis=0, concat_axis=0, tiled=True)
    arrived_other = swapped(arrived, "walk", 0)
    first = bias_half(core, arrived, kept, jnp.zeros((owners, held), f32), 1)
    spread = bias_half(1 - core, arrived_other, kept, first[0], owners)
    parts = lax.all_to_all(spread, axes, split_axis=0, concat_axis=0, tiled=True)
    force_bias, send = potential_half(1 - core, parts, field_noise[0], kept)
    _, keep = potential_half(core, parts, field_noise[0], kept)
    summed = jnp.swapaxes((keep + swapped(send, "walk", 0)).astype(bf16), 0, 1)
    received = lax.all_to_all(summed, axes, split_axis=0, concat_axis=0, tiled=True)
    received_other = swapped(received, "walk", 0)
    sizes = dict(row_groups=row_groups, col_groups=col_groups)
    width = own.shape[1]
    prepared = pl.pallas_call(
        functools.partial(joined_body, **sizes),
        out_shape=(
            jax.ShapeDtypeStruct((SUBS * row_groups, SUB // 2, 2 * SUB * col_groups), bf16),
            jax.ShapeDtypeStruct((width, orbital_count), f32),
            jax.ShapeDtypeStruct((2 * width, orbital_count), bf16),
        ),
        in_specs=[vmem, vmem],
        out_specs=(vmem, vmem, vmem),
        compiler_params=grant,
        name="joined",
    )(received, own)
    propagated = pl.pallas_call(
        functools.partial(series_body, **sizes),
        out_shape=jax.ShapeDtypeStruct(own.shape, f32),
        in_specs=[smem, vmem, vmem, vmem, vmem],
        out_specs=anywhere,
        scratch_shapes=[
            pltpu.VMEM((orbital_count, orbital_count), bf16),
            pltpu.VMEM(own.shape, f32),
            pltpu.SemaphoreType.DMA((SUBS * row_groups,)),
        ],
        compiler_params=grant,
        name="series",
    )(core, *prepared, received_other)
    return propagated[None], force_bias[None]


def packable(chol_vectors, trial_orbitals, walkers, field_noise):
    held, slab_rows, slab_cols = chol_vectors.shape
    row_groups = lax.axis_size("pairs")
    return (
        walkers.shape[0] == 1
        and lax.axis_size("walk") == 2
        and lax.axis_size("chol") == row_groups
        and row_groups in (2, 4, 8)
        and slab_cols == slab_rows == SUB * SUBS
        and held % LANES == 0
        and trial_orbitals.shape[1] % LANES == 0
        and field_noise.shape[0] == 1
    )


def chosen_shards(*args):
    return fast_shards(*args) if packable(*args) else shards(*args)


def solution(mesh):
    placed = (
        P(("groups", "walk"), "pairs", "chol"),
        P("groups", None),
        P(("groups", "pairs", "chol"), None, "walk"),
        P("groups", None, "walk"),
    )
    return jax.shard_map(
        chosen_shards,
        mesh=mesh,
        in_specs=placed,
        out_specs=(P(("groups", "pairs", "chol"), None, "walk"), P("groups", None, "walk")),
        check_vma=False,
    )
```

```python
import functools

import jax
import jax.numpy as jnp
from jax import lax
from jax.experimental import pallas as pl
from jax.experimental.pallas import tpu as pltpu
from jax.sharding import PartitionSpec as P

TERMS = 6


root_step = 0.05
highest = lax.Precision.HIGHEST
LANES = 128
SUB = LANES // 2
SUBS = 3
f32 = jnp.float32
bf16 = jnp.bfloat16


def swapped(value, axis, apart):
    mask = 2**apart
    pairs = [(source, source ^ mask) for source in range(lax.axis_size(axis))]
    return lax.ppermute(value, axis, pairs)


def solve_normal(factor, right_side):
    middle = lax.linalg.triangular_solve(factor, right_side, left_side=True, lower=True)
    return lax.linalg.triangular_solve(factor, middle, left_side=True, lower=True, transpose_a=True)


def green_blocks(walker_full, trial_orbitals, trial_part, row_groups, col_groups):
    owner_walkers, orbital_count, electron_count = walker_full.shape
    intersection = jnp.einsum("nm,wnk->wmk", trial_orbitals, walker_full, precision=highest)
    normal = jnp.einsum("wmk,wml->wkl", intersection, intersection, precision=highest)
    factor = jnp.linalg.cholesky(normal)
    rotated = jnp.einsum("wmk,cbm->wkcb", intersection, trial_part, precision=highest)
    chosen_cols = rotated.shape[2] * rotated.shape[3]
    solved = solve_normal(factor, rotated.reshape(owner_walkers, electron_count, chosen_cols))
    slab_rows = orbital_count // row_groups
    block_cols = chosen_cols // col_groups
    shaped = solved.reshape(owner_walkers, electron_count, col_groups, block_cols)
    walker_rows = walker_full.reshape(owner_walkers, row_groups, slab_rows, electron_count)
    blocks = jnp.einsum("wiak,wkcb->icwab", walker_rows, shaped, precision=highest)
    return blocks.astype(jnp.bfloat16).reshape(
        row_groups * col_groups, owner_walkers, slab_rows * block_cols
    )


def shards(chol_vectors, trial_orbitals, walkers, field_noise):
    held_vectors, slab_rows, slab_cols = chol_vectors.shape
    owner_walkers = walkers.shape[0]
    orbital_count = walkers.shape[1]
    electron_count = trial_orbitals.shape[1]
    row_groups = lax.axis_size("pairs")
    col_groups = lax.axis_size("chol")
    core_count = lax.axis_size("walk")
    core_index = lax.axis_index("walk")
    core_cols = slab_cols // core_count
    owner_count = row_groups * col_groups
    walker_total = owner_count * owner_walkers
    flat_vectors = chol_vectors.reshape(held_vectors, slab_rows * slab_cols)
    trial_split = trial_orbitals.reshape(col_groups, core_count, core_cols, electron_count)
    trial_part = lax.dynamic_index_in_dim(trial_split, core_index, 1, keepdims=False)
    walker_full = lax.all_gather(walkers, "walk", axis=2, tiled=True)
    outgoing = green_blocks(walker_full, trial_orbitals, trial_part, row_groups, col_groups)
    sectioned = outgoing.reshape(row_groups, col_groups, owner_walkers, slab_rows * core_cols)
    arrived = lax.all_to_all(
        lax.all_to_all(sectioned, "pairs", split_axis=0, concat_axis=0, tiled=True),
        "chol",
        split_axis=1,
        concat_axis=1,
        tiled=True,
    )
    arrived = arrived.reshape(walker_total, slab_rows, core_cols)
    partial_bias = jnp.einsum(
        "wab,gab->wg",
        lax.all_gather(arrived, "walk", axis=2, tiled=True),
        chol_vectors,
        preferred_element_type=jnp.float32,
    )
    force_bias = lax.psum(partial_bias, ("pairs", "chol"))
    bias_steps = [force_bias]
    shifted = field_noise[0] + root_step * force_bias
    shifted_high = lax.optimization_barrier(shifted.astype(jnp.bfloat16))
    shifted_low = (shifted - shifted_high.astype(jnp.float32)).astype(jnp.bfloat16)
    stacked = jnp.stack([shifted_high, shifted_low])
    both_parts = lax.dot_general(
        stacked, flat_vectors, (((2,), (0,)), ((), ())), preferred_element_type=jnp.float32
    )
    potential = both_parts[0] + both_parts[1]
    blocks_out = potential.reshape(owner_count, owner_walkers, slab_rows * slab_cols)
    received = lax.all_to_all(
        blocks_out, ("pairs", "chol"), split_axis=0, concat_axis=0, tiled=True
    )
    partner = swapped(received, "walk", 0)
    summed = (received + partner).reshape(
        row_groups, col_groups, owner_walkers, slab_rows, core_count, core_cols
    )
    matrix = jnp.transpose(summed, (2, 0, 3, 1, 4, 5)).reshape(
        owner_walkers, orbital_count, orbital_count
    )
    running_term = walkers
    running_sum = walkers
    for degree in range(1, TERMS):
        running_term = -(root_step / degree) * jnp.einsum(
            "wpq,wqm->wpm", matrix, running_term, precision=highest
        )
        running_sum = running_sum + running_term
    return (running_sum, jnp.stack(bias_steps))


def split_two(value):
    high = value.astype(bf16)
    return high, (value - high.astype(f32)).astype(bf16)


def dot_of(left, right, dims=(((1,), (0,)), ((), ())), precision=None):
    return lax.dot_general(left, right, dims, precision=precision, preferred_element_type=f32)


def dot_three(left, right):
    left_high, left_low = split_two(left)
    right_high, right_low = split_two(right)
    return dot_of(
        jnp.concatenate([left_high, left_low, left_high], axis=1),
        jnp.concatenate([right_high, right_high, right_low], axis=0),
    )


first_dims = (((0,), (0,)), ((), ()))
last_dims = (((1,), (1,)), ((), ()))


def eye_of(size):
    rows = lax.broadcasted_iota(jnp.int32, (size, size), 0)
    cols = lax.broadcasted_iota(jnp.int32, (size, size), 1)
    return (rows == cols).astype(f32)


def half_rolled(value):
    return pltpu.roll(value, LANES // 2, 1)


def tail_lanes(value):
    return lax.broadcasted_iota(jnp.int32, value.shape, 1) < LANES // 2


LOW_START = 4e-4
PAIRED_STEPS = 7
RESIDUAL_BOUND = 2e-2
MOST_STEPS = 60


def scales():
    low = LOW_START
    found = []
    for _ in range(PAIRED_STEPS + 1):
        scale = 2.0 / (1.0 + 2.0 * low - low * low)
        found.append(scale)
        low = 2.0 - scale
    return found


def three_terms(left, right, dims=(((1,), (0,)), ((), ()))):
    count = left[0].shape[0]
    both = dot_of(jnp.concatenate(left, axis=0), right[0], dims)
    return both[:count] + both[count:] + dot_of(left[0], right[1], dims)


def overlap_body(own_ref, trial_ref, inter_ref, turned_high_ref, turned_low_ref, high_ref, low_ref, own_high_ref, own_low_ref):
    trial = trial_ref[...]
    own = split_two(own_ref[...])
    turned = split_two(trial.T)
    inter_ref[...] = three_terms(turned, own)
    turned_high_ref[...], turned_low_ref[...] = turned
    high_ref[...], low_ref[...] = split_two(trial)
    own_high_ref[...], own_low_ref[...] = own


def green_body(
    core_ref, other_ref, inter_ref, turned_high_ref, turned_low_ref, high_ref, low_ref, own_high_ref,
    own_low_ref, vector_ref, out_ref, kept_ref, inverse_ref, matrix_ref,
    solved_high_ref, solved_low_ref, sems, *, row_groups, col_groups
):
    core = core_ref[0]
    odd = core_ref[1]
    copies = []
    for sub in range(SUBS):
        rows = pl.ds(sub * SUB, SUB)
        for beside in range(2):
            cols = pl.ds((sub + beside) % SUBS * SUB, SUB)
            target = odd if beside == 0 else 1 - odd
            copies.append(
                pltpu.make_async_copy(
                    vector_ref.at[rows, cols, :],
                    kept_ref.at[rows, pl.ds(pl.multiple_of(target * SUB, SUB), SUB), :],
                    sems.at[2 * sub + beside],
                )
            )
            copies[-1].start()
    orbital_count, electron_count = high_ref.shape
    slab_rows = orbital_count // row_groups
    slab_cols = orbital_count // col_groups
    other = split_two(other_ref[...])
    inter_other = three_terms((turned_high_ref[...], turned_low_ref[...]), other)
    inter = jnp.concatenate([inter_ref[...], inter_other], axis=1)
    inverse_scale = 1.0 / jnp.max(jnp.abs(inter))
    inter = inter * inverse_scale
    matrix_ref[...] = inter
    turned = inter.T
    eye = eye_of(electron_count)
    normal = dot_three(turned, inter)
    both = dot_three(normal, jnp.concatenate([normal, turned], axis=1))
    square = both[:, :electron_count]
    step_scales = scales()
    largest = jnp.sqrt(jnp.sqrt(jnp.sum(square * square))) * 1.001
    alpha = (2.0 - LOW_START) / largest
    scale = step_scales[0]
    error = eye - (2.0 * scale * alpha) * normal + (scale * alpha * alpha) * square
    inverse = (scale * alpha) * (2.0 * turned - alpha * both[:, electron_count:])
    for scale in step_scales[1:-1]:
        both = dot_three(error, jnp.concatenate([error, inverse], axis=1))
        inverse = scale * (inverse + both[:, electron_count:])
        error = (1.0 - scale) * eye + scale * both[:, :electron_count]
    inverse_ref[...] = step_scales[-1] * (inverse + dot_three(error, inverse))

    def refine(carried):
        count, _ = carried
        current = inverse_ref[...]
        residual = eye_of(electron_count) - dot_three(current, matrix_ref[...])
        inverse_ref[...] = current + dot_three(residual, current)
        return count + 1, jnp.sum(residual * residual)

    lax.while_loop(
        lambda carried: jnp.logical_and(carried[0] < MOST_STEPS, carried[1] > RESIDUAL_BOUND**2),
        refine,
        (jnp.int32(0), jnp.float32(1e30)),
    )
    walker = [
        jnp.concatenate([own, there], axis=1)
        for own, there in zip((own_high_ref[...], own_low_ref[...]), other)
    ]
    inverse = inverse_ref[...] * inverse_scale
    solved_high_ref[...], solved_low_ref[...] = split_two(three_terms(walker, split_two(inverse)))
    part = SUB // 2
    trial_refs = (high_ref, low_ref)
    solved_refs = (solved_high_ref, solved_low_ref)
    for sub in range(SUBS):
        following = (sub + 1) % SUBS
        starts = [
            pl.multiple_of(row * slab_rows + sub * SUB + core * part, part) for row in range(row_groups)
        ]
        same = [col * slab_cols + sub * SUB for col in range(col_groups)]
        beside = [col * slab_cols + following * SUB for col in range(col_groups)]
        mixed = []
        for col in range(col_groups):
            mixed += [beside[col], same[col]] if col % 2 else [same[col], beside[col]]

        def rows_of(refs, places, size):
            return [jnp.concatenate([ref[pl.ds(at, size), :] for at in places], axis=0) for ref in refs]

        green = three_terms(
            rows_of(solved_refs, starts, part), rows_of(trial_refs, mixed, SUB), last_dims
        )
        turned = three_terms(
            rows_of(trial_refs, starts, part), rows_of(solved_refs, beside, SUB), last_dims
        )
        for col in range(col_groups):
            tile = green[:, col * LANES : (col + 1) * LANES].astype(bf16).astype(f32)
            lane = col // 2 * LANES
            added = half_rolled(turned[:, lane : lane + LANES]).astype(bf16).astype(f32)
            first = tail_lanes(tile)
            plain, summed = tile, tile + added
            summed = jnp.where(first, summed, plain) if col % 2 else jnp.where(first, plain, summed)
            summed = summed.astype(bf16)
            for row in range(row_groups):
                out_ref[row * col_groups + col, sub * part : (sub + 1) * part, :] = summed[
                    row * part : (row + 1) * part
                ]
    for copy in copies:
        copy.wait()


def kept_rows(kept_ref, sub, place):
    part = SUB // 2
    start = pl.multiple_of(sub * SUB + place * part, part)
    return kept_ref[pl.ds(start, part)].reshape(part * LANES, kept_ref.shape[2])


def bias_body(place_ref, green_ref, kept_ref, before_ref, out_ref, turned_ref):
    part = SUB // 2
    place = place_ref[0]
    turned_ref[...] = jnp.swapaxes(green_ref[...].astype(f32), 0, 1).astype(bf16)
    total = before_ref[...]
    for sub in range(SUBS):
        left = [turned_ref[sub * part + row] for row in range(part)]
        total = total + dot_of(jnp.concatenate(left, axis=1), kept_rows(kept_ref, sub, place))
    for device in range(out_ref.shape[0]):
        out_ref[device] = total


def potential_body(place_ref, parts_ref, noise_ref, kept_ref, bias_ref, out_ref):
    part = SUB // 2
    place = place_ref[0]
    walker_total = noise_ref.shape[0]
    bias = parts_ref[0]
    for device in range(1, parts_ref.shape[0]):
        bias = bias + parts_ref[device]
    bias_ref[...] = bias
    high, low = split_two(noise_ref[...] + root_step * bias)
    weights = jnp.concatenate([high, low], axis=0)
    for sub in range(SUBS):
        both = dot_of(weights, kept_rows(kept_ref, sub, place), last_dims)
        added = both[:walker_total] + both[walker_total:]
        for row in range(part):
            out_ref[sub * part + row] = added[:, row * LANES : (row + 1) * LANES]


def joined_tiles(source_ref, sub, row, col_groups):
    part = SUB // 2
    same = []
    beside = []
    for col in range(0, col_groups, 2):
        index = row * col_groups + col
        even = source_ref[index, sub * part : (sub + 1) * part, :]
        odd = source_ref[index + 1, sub * part : (sub + 1) * part, :]
        same.append(jnp.where(tail_lanes(even), even, odd))
        beside.append(half_rolled(jnp.where(tail_lanes(even), odd, even).astype(f32)).astype(bf16))
    return jnp.concatenate(same + beside, axis=1)


def joined_body(source_ref, walker_ref, out_ref, turned_ref, pair_ref, *, row_groups, col_groups):
    for sub in range(SUBS):
        for row in range(row_groups):
            out_ref[sub * row_groups + row] = joined_tiles(source_ref, sub, row, col_groups)
    slab = SUB * SUBS
    pieces = []
    for sub in range(SUBS):
        for row in range(row_groups):
            pieces.append(walker_ref[row * slab + sub * SUB : row * slab + (sub + 1) * SUB, :])
    term = jnp.concatenate(pieces, axis=0).T
    turned_ref[...] = term
    pair_ref[...] = jnp.concatenate(split_two(term), axis=0)


def series_body(core_ref, joined_ref, turned_ref, pair_ref, other_ref, out_ref, matrix_ref, stage_ref, sems, *, row_groups, col_groups):
    slab = SUB * SUBS
    part = SUB // 2
    size = row_groups * SUB
    core = core_ref[0]
    for place in range(2):
        for sub in range(SUBS):
            lane = (sub + 1) % SUBS * size
            for row in range(row_groups):
                if place == 0:
                    tiles = joined_ref[sub * row_groups + row]
                    shift = core * part
                else:
                    tiles = joined_tiles(other_ref, sub, row, col_groups)
                    shift = (1 - core) * part
                rows = pl.ds(pl.multiple_of(sub * size + row * SUB + shift, part), part)
                matrix_ref[rows, sub * size : (sub + 1) * size] = tiles[:, :size]
                matrix_ref[rows, lane : lane + size] = tiles[:, size:]
    for sub in range(SUBS):
        following = (sub + 1) % SUBS
        block = matrix_ref[sub * size : (sub + 1) * size, following * size : (following + 1) * size]
        matrix_ref[following * size : (following + 1) * size, sub * size : (sub + 1) * size] = block.T

    total = turned_ref[...]
    count = total.shape[0]
    left = pair_ref[...]
    for degree in range(1, TERMS):
        both = dot_of(left, matrix_ref[...])
        if degree < 2:
            both = both[:count] + both[count:]
        term = (-root_step / degree) * both
        total = total + term
        left = term.astype(bf16)
    copies = []
    for sub in range(SUBS):
        rows = slice(sub * size, (sub + 1) * size)
        stage_ref[rows, :] = total[:, rows].T
        for row in range(row_groups):
            copies.append(
                pltpu.make_async_copy(
                    stage_ref.at[pl.ds(sub * size + row * SUB, SUB), :],
                    out_ref.at[pl.ds(row * slab + sub * SUB, SUB), :],
                    sems.at[sub * row_groups + row],
                )
            )
            copies[-1].start()
    for copy in copies:
        copy.wait()


smem = pl.BlockSpec(memory_space=pltpu.SMEM)
vmem = pl.BlockSpec(memory_space=pltpu.VMEM)
anywhere = pl.BlockSpec(memory_space=pl.ANY)
grant = pltpu.CompilerParams(vmem_limit_bytes=20 * 2**20)


def bias_half(place, green, kept, before, copies):
    owners, dense, _ = green.shape
    held = kept.shape[2]
    return pl.pallas_call(
        bias_body,
        in_specs=[smem, vmem, vmem, vmem],
        out_specs=vmem,
        scratch_shapes=[pltpu.VMEM((dense, owners, LANES), bf16)],
        out_shape=jax.ShapeDtypeStruct((copies, owners, held), f32),
        compiler_params=grant,
        name="bias",
    )(place, green, in_vmem(kept), before)


def in_hbm(value):
    return pltpu.with_memory_space_constraint(value, pltpu.HBM)


def in_vmem(value):
    return pltpu.with_memory_space_constraint(value, pltpu.VMEM)


def potential_half(place, parts, noise, kept):
    _, owners, held = parts.shape
    return pl.pallas_call(
        potential_body,
        in_specs=[smem, vmem, vmem, vmem],
        out_specs=(vmem, vmem),
        out_shape=(
            jax.ShapeDtypeStruct((owners, held), f32),
            jax.ShapeDtypeStruct((SUBS * SUB // 2, owners, LANES), f32),
        ),
        compiler_params=grant,
        name="potential",
    )(place, parts, noise, in_vmem(kept))


def fast_shards(chol_vectors, trial_orbitals, walkers, field_noise):
    held = chol_vectors.shape[0]
    orbital_count, electron_count = trial_orbitals.shape
    row_groups = lax.axis_size("pairs")
    col_groups = lax.axis_size("chol")
    owners = row_groups * col_groups
    dense = SUBS * SUB // 2
    core = lax.axis_index("walk").astype(jnp.int32).reshape(1)
    parity = (lax.axis_index("chol").astype(jnp.int32) % 2).reshape(1)
    vectors = jnp.transpose(chol_vectors, (1, 2, 0))
    own = walkers[0]
    other = swapped(own, "walk", 0)
    early = pl.pallas_call(
        overlap_body,
        out_shape=[jax.ShapeDtypeStruct((electron_count, own.shape[1]), f32)]
        + [jax.ShapeDtypeStruct((electron_count, orbital_count), bf16)] * 2
        + [jax.ShapeDtypeStruct(trial_orbitals.shape, bf16)] * 2
        + [jax.ShapeDtypeStruct(own.shape, bf16)] * 2,
        in_specs=[vmem, vmem],
        out_specs=[vmem] * 7,
        compiler_params=grant,
        name="overlap",
    )(in_hbm(own), in_hbm(trial_orbitals))
    square = (electron_count, electron_count)
    outgoing, kept = pl.pallas_call(
        functools.partial(green_body, row_groups=row_groups, col_groups=col_groups),
        out_shape=(
            jax.ShapeDtypeStruct((owners, dense, LANES), bf16),
            pltpu.VMEM((SUBS * SUB, LANES, held), bf16),
        ),
        in_specs=[smem] + [vmem] * 8 + [anywhere],
        out_specs=(vmem, vmem),
        scratch_shapes=[
            pltpu.VMEM(square, f32),
            pltpu.VMEM(square, f32),
            pltpu.VMEM(trial_orbitals.shape, bf16),
            pltpu.VMEM(trial_orbitals.shape, bf16),
            pltpu.SemaphoreType.DMA((2 * SUBS,)),
        ],
        compiler_params=grant,
        name="green",
    )(jnp.concatenate([core, parity]), other, *early, in_hbm(vectors))
    axes = ("pairs", "chol")
    arrived = lax.all_to_all(outgoing, axes, split_axis=0, concat_axis=0, tiled=True)
    arrived_other = swapped(arrived, "walk", 0)
    first = bias_half(core, arrived, kept, jnp.zeros((owners, held), f32), 1)
    spread = bias_half(1 - core, arrived_other, kept, first[0], owners)
    parts = lax.all_to_all(spread, axes, split_axis=0, concat_axis=0, tiled=True)
    force_bias, send = potential_half(1 - core, parts, field_noise[0], kept)
    _, keep = potential_half(core, parts, field_noise[0], kept)
    summed = jnp.swapaxes((keep + swapped(send, "walk", 0)).astype(bf16), 0, 1)
    received = lax.all_to_all(summed, axes, split_axis=0, concat_axis=0, tiled=True)
    received_other = swapped(received, "walk", 0)
    sizes = dict(row_groups=row_groups, col_groups=col_groups)
    width = own.shape[1]
    prepared = pl.pallas_call(
        functools.partial(joined_body, **sizes),
        out_shape=(
            jax.ShapeDtypeStruct((SUBS * row_groups, SUB // 2, 2 * SUB * col_groups), bf16),
            jax.ShapeDtypeStruct((width, orbital_count), f32),
            jax.ShapeDtypeStruct((2 * width, orbital_count), bf16),
        ),
        in_specs=[vmem, vmem],
        out_specs=(vmem, vmem, vmem),
        compiler_params=grant,
        name="joined",
    )(received, own)
    propagated = pl.pallas_call(
        functools.partial(series_body, **sizes),
        out_shape=jax.ShapeDtypeStruct(own.shape, f32),
        in_specs=[smem, vmem, vmem, vmem, vmem],
        out_specs=anywhere,
        scratch_shapes=[
            pltpu.VMEM((orbital_count, orbital_count), bf16),
            pltpu.VMEM(own.shape, f32),
            pltpu.SemaphoreType.DMA((SUBS * row_groups,)),
        ],
        compiler_params=grant,
        name="series",
    )(core, *prepared, received_other)
    return propagated[None], force_bias[None]


def packable(chol_vectors, trial_orbitals, walkers, field_noise):
    held, slab_rows, slab_cols = chol_vectors.shape
    row_groups = lax.axis_size("pairs")
    return (
        walkers.shape[0] == 1
        and lax.axis_size("walk") == 2
        and lax.axis_size("chol") == row_groups
        and row_groups in (2, 4, 8)
        and slab_cols == slab_rows == SUB * SUBS
        and held % LANES == 0
        and trial_orbitals.shape[1] % LANES == 0
        and field_noise.shape[0] == 1
    )


def chosen_shards(*args):
    return fast_shards(*args) if packable(*args) else shards(*args)


def solution(mesh):
    placed = (
        P(("groups", "walk"), "pairs", "chol"),
        P("groups", None),
        P(("groups", "pairs", "chol"), None, "walk"),
        P("groups", None, "walk"),
    )
    return jax.shard_map(
        chosen_shards,
        mesh=mesh,
        in_specs=placed,
        out_specs=(P(("groups", "pairs", "chol"), None, "walk"), P("groups", None, "walk")),
        check_vma=False,
    )
```
